32 devices in a mesh: blk: 8 (over z, x), rows: 4 (over y, core).
Axes of the slice: x: 2, y: 2, z: 4, core: 2. Of those that a mesh axis runs over, the one named last changes fastest.
Arguments:
- patterns: bfloat16 [2048, 4096], P('blk', 'rows'), may hold values from -6 to 6
- dictionary: bfloat16 [16384, 4096], P('blk', 'rows'), may hold values from -6 to 6
- codes: bfloat16 [2048, 256], P('blk'), may hold values from -6 to 6
- support: int32 [2048, 4], P('blk'), may hold values from 0 to 7, all different within a row
- wanted: int32 [8, 8], P('blk'), may hold values from 0 to 31
Outputs:
- dictionary_out: bfloat16 [16384, 4096], P('blk', 'rows')
- codes_out: float32 [2048, 256], P('blk')
The draws below stay inside these ranges and needn't reach their ends.
Inputs may be any that keep to these rules, and one draw needn't show every extreme that they name: `support`: the 4 entries of a row are different, and every slot is named by some pattern.
All inputs are finite; a program needn't handle non-finite values.
Results may differ from the reference program's by a relative error of at most 0.014.
Values may be sent and summed in bfloat16 or wider, within the bound.
A program may use at most 64 MiB of HBM per device.

```python
import jax
import jax.numpy as jnp
from jax import lax

PIXELS = 4096
BLOCK = 64
ABLK_DEV = 32
SUPP = 4
P_DEV = 256
REGIONS = 8
PATTERNS = 2048
ATOMS = 16384
N_BLK = 8


def plant(array, rng, low, high):
    index_at = [jax.random.randint(jax.random.fold_in(rng, axis), (), 0, length) for axis, length in enumerate(array.shape)]
    main_axis = array.shape.index(max(array.shape))
    neighbour = index_at[:main_axis] + [(index_at[main_axis] + 1) % array.shape[main_axis]] + index_at[main_axis + 1:]
    return array.at[tuple(index_at)].set(low).at[tuple(neighbour)].set(high)


def shard_levels(key, extent, pieces, low, high):
    level = 1.0
    for axis_at, parts in pieces:
        draws = jax.random.uniform(jax.random.fold_in(jax.random.fold_in(key, 6), axis_at), (parts,), jnp.float32, low / len(pieces), high / len(pieces))
        level = level * jnp.repeat(jnp.exp(draws), extent[axis_at] // parts).reshape((-1,) + (1,) * (len(extent) - 1 - axis_at))
    return level


def different_ones(stream_key, rows, amount, top, lift):
    sequence = jax.random.permutation(jax.random.fold_in(stream_key, 1), amount)
    pull = sequence
    for power in range(3):
        pull = pull * pull // amount
    pull = pull * lift // amount
    chance = jax.random.randint(jax.random.fold_in(stream_key, 2), (rows, amount), 0, 4096) + pull
    fixed_rows = jax.random.permutation(jax.random.fold_in(stream_key, 3), rows)[jnp.arange(amount) % rows]
    chance = jnp.where(jnp.arange(rows)[:, None] == fixed_rows[None, :], 1 << 14, chance)
    score = chance * amount + jnp.arange(amount)
    return lax.top_k(score.astype(jnp.int32), top)[1].astype(jnp.int32)


def normal_values(stream_key, dims, width, reach, shards=(), kind=jnp.bfloat16):
    result = width * jax.random.normal(stream_key, dims, jnp.float32)
    if shards:
        result = result * shard_levels(stream_key, dims, shards, -0.22, 0.18)
    return jnp.clip(result, -reach, reach).astype(kind)


def setup_inputs(seed: int = 0) -> dict:
    splits = jax.random.split(jax.random.key(seed), 6)
    return {
        "patterns": normal_values(splits[0], (PATTERNS, PIXELS), 1.0, 6.0, ((0, 8), (1, 4))),
        "dictionary": normal_values(splits[1], (ATOMS, PIXELS), 1.0, 6.0, ((0, 8), (1, 4))),
        "codes": normal_values(splits[2], (PATTERNS, SUPP * BLOCK), 1.0, 6.0, ((0, 8),)),
        "support": different_ones(splits[3], PATTERNS, N_BLK, SUPP, 8192),
        "wanted": plant(jax.random.randint(splits[4], (REGIONS, N_BLK), 0, ABLK_DEV), jax.random.fold_in(splits[4], 1), 0, ABLK_DEV - 1).astype(jnp.int32),
    }


CODE_RATE = 0.05
ATOM_RATE = 0.2


def reference(patterns, dictionary, codes, support, wanted):
    scale_factor = (SUPP * BLOCK) ** -0.5
    total_blocks = ABLK_DEV * N_BLK
    slot_ids = jnp.arange(N_BLK, dtype=jnp.int32)
    block_ids = (slot_ids[None, :] * ABLK_DEV + wanted).astype(jnp.int32)
    pattern_regions = patterns.reshape(N_BLK, P_DEV, PIXELS)
    support_regions = support.reshape(N_BLK, P_DEV, SUPP)
    atoms_now = dictionary
    codes_now = codes
    for step_index in range(2):
        blocks_now = atoms_now.reshape(total_blocks, BLOCK, PIXELS)
        code_regions = codes_now.astype(jnp.bfloat16).reshape(N_BLK, P_DEV, SUPP, BLOCK)

        def region_work(carry, items):
            region_rows, region_codes, region_support, region_blocks = items
            panels = jnp.take(blocks_now, region_blocks, axis=0).reshape(N_BLK * BLOCK, PIXELS)
            picker = (region_support[:, :, None] == slot_ids[None, None, :]).astype(jnp.float32)
            dense = jnp.einsum("psn,pse->pne", picker, region_codes.astype(jnp.float32),
                               precision=lax.Precision.HIGHEST)
            dense = dense.astype(jnp.bfloat16).reshape(P_DEV, N_BLK * BLOCK)
            rebuilt = scale_factor * jnp.dot(dense, panels, preferred_element_type=jnp.float32)
            residual = (region_rows.astype(jnp.float32) - rebuilt).astype(jnp.bfloat16)
            correlated = jnp.dot(residual, panels.T, preferred_element_type=jnp.float32)
            code_grad = scale_factor * jnp.einsum("psn,pne->pse", picker,
                                                  correlated.reshape(P_DEV, N_BLK, BLOCK),
                                                  precision=lax.Precision.HIGHEST)
            atom_terms = scale_factor * jnp.dot(dense.T, residual, preferred_element_type=jnp.float32)
            carry = carry.at[region_blocks].add(atom_terms.reshape(N_BLK, BLOCK, PIXELS))
            return carry, code_grad

        grad_start = jnp.zeros((total_blocks, BLOCK, PIXELS), jnp.float32)
        atom_grad, code_grads = lax.scan(region_work, grad_start,
                                         (pattern_regions, code_regions, support_regions, block_ids))
        atoms_now = (atoms_now.astype(jnp.float32)
                     + ATOM_RATE * atom_grad.reshape(ATOMS, PIXELS)).astype(jnp.bfloat16)
        codes_now = codes_now.astype(jnp.float32) + CODE_RATE * code_grads.reshape(PATTERNS, SUPP * BLOCK)
    return atoms_now, codes_now
```

```python
import functools

import jax
import jax.numpy as jnp
from jax import lax
from jax.experimental import pallas as pl
from jax.experimental.pallas import tpu as pltpu
from jax.sharding import PartitionSpec as P

CODE_RATE = 0.05
ATOM_RATE = 0.2
LANES = 128
MESH = pl.DeviceIdType.MESH
F32 = jnp.float32
BF16 = jnp.bfloat16
FIRST_TO_FIRST = (((0,), (0,)), ((), ()))
LAST_TO_LAST = (((1,), (1,)), ((), ()))


def steps_kernel(
    owners, row_count, group, block_width, scale_factor,
    wanted_hbm, support_hbm, codes_hbm, patterns_hbm, dictionary_hbm,
    dictionary_out, codes_out,
    pool, patterns_ref, codes_ref, support_all, asked_vmem, asked_smem, chosen,
    codes_all, staged, panels, pixels, dense, spare, residuals, terms, sums, products,
    far_terms, panels_next, residuals_next, term_out, arrived, totals,
    part_out, part_in, row_parts, master, codes_next,
    load_sems, ask_send, ask_recv, support_send, support_recv,
    codes_send, codes_recv, far_send, far_recv, fan_send, fan_recv, lift_send, lift_recv,
    pixel_send, pixel_recv, panel_send, panel_recv, residual_send, residual_recv,
    part_send, part_recv, row_send, row_recv, next_send, next_recv, term_send, term_recv,
):
    me = lax.axis_index("blk")
    my_row = lax.axis_index("rows")
    groups = owners // group
    mine = me // group
    spot = lax.rem(me, group)
    base = mine * group
    owned = dictionary_out.shape[0]
    pattern_rows, pixel_count = patterns_ref.shape
    support_count = support_hbm.shape[0]
    code_width = codes_ref.shape[1]
    width = pixel_count // group
    share = code_width // row_count
    share_rows = pl.ds(pl.multiple_of(my_row * share, share), share)

    def columns(k):
        return pl.ds(pl.multiple_of(k * width, width), width)

    loads = (
        pltpu.make_async_copy(wanted_hbm, asked_vmem.at[me], load_sems.at[0]),
        pltpu.make_async_copy(support_hbm, support_all.at[me], load_sems.at[1]),
        pltpu.make_async_copy(codes_hbm, codes_ref, load_sems.at[2]),
        pltpu.make_async_copy(dictionary_hbm, pool.at[pl.ds(0, owned)], load_sems.at[3]),
        pltpu.make_async_copy(patterns_hbm, patterns_ref, load_sems.at[4]),
    )
    for load in loads:
        load.start()

    barrier = pltpu.get_barrier_semaphore()
    for j in range(1, owners):
        pl.semaphore_signal(
            barrier, inc=1, device_id={"blk": lax.rem(me + j, owners)}, device_id_type=MESH
        )
    for j in range(1, row_count):
        pl.semaphore_signal(
            barrier, inc=1, device_id={"rows": lax.rem(my_row + j, row_count)}, device_id_type=MESH
        )
    pl.semaphore_wait(barrier, owners + row_count - 2)

    def remote(source, target, send, recv, device):
        return pltpu.make_async_remote_copy(
            src_ref=source, dst_ref=target, send_sem=send, recv_sem=recv,
            device_id=device, device_id_type=MESH,
        )

    def peer(j):
        return lax.rem(me + j, owners)

    def beside(k):
        return lax.rem(spot + k, group)

    def other(h):
        return lax.rem(mine + h, groups)

    def row_peer(j):
        return {"rows": lax.rem(my_row + j, row_count)}

    def ask_copy(j):
        return remote(asked_vmem.at[me], asked_vmem.at[me], ask_send.at[j], ask_recv.at[j],
                      {"blk": peer(j)})

    def support_copy(j):
        return remote(support_all.at[me], support_all.at[me], support_send.at[j],
                      support_recv.at[j], {"blk": peer(j)})

    def codes_copy(k):
        return remote(codes_all.at[me], codes_all.at[me], codes_send.at[k], codes_recv.at[k],
                      {"blk": base + beside(k)})

    def far_copy(h):
        piece = codes_all.at[me, share_rows]
        return remote(piece, piece, far_send.at[h], far_recv.at[h],
                      {"blk": other(h) * group + spot})

    def fan_copy(h, k):
        piece = codes_all.at[other(h) * group + spot, share_rows]
        return remote(piece, piece, fan_send.at[h, k], fan_recv.at[h, k],
                      {"blk": base + beside(k)})

    def lift_copy(h, j):
        piece = codes_all.at[pl.ds(other(h) * group, group), share_rows]
        return remote(piece, piece, lift_send.at[h, j], lift_recv.at[h, j], row_peer(j))

    def pixel_copy(k):
        return remote(patterns_ref.at[:, columns(beside(k))], pixels.at[spot],
                      pixel_send.at[k], pixel_recv.at[k], {"blk": base + beside(k)})

    def panel_copy(a, j):
        to = peer(j)
        return remote(staged.at[lax.rem(to, group), (to // group) * group + a],
                      panels.at[a, me], panel_send.at[a, j], panel_recv.at[a, j], {"blk": to})

    def residual_copy(a, h):
        piece = residuals.at[base + a]
        return remote(piece, piece, residual_send.at[a, h], residual_recv.at[a, h],
                      {"blk": other(h) * group + spot})

    def part_copy(step, k):
        return remote(part_out.at[step, beside(k)], part_in.at[step, spot],
                      part_send.at[step, k], part_recv.at[step, k], {"blk": base + beside(k)})

    def row_copy(step, j):
        piece = row_parts.at[step, my_row]
        return remote(piece, piece, row_send.at[step, j], row_recv.at[step, j], row_peer(j))

    def next_copy(k):
        return remote(codes_next.at[spot], codes_next.at[spot], next_send.at[k], next_recv.at[k],
                      {"blk": base + beside(k)})

    def term_copy(a, j):
        to = peer(j)
        return remote(term_out.at[a, to], arrived.at[base + a, spot],
                      term_send.at[a, j], term_recv.at[a, j], {"blk": to})

    loads[0].wait()
    for j in range(1, owners):
        ask_copy(j).start()
    loads[1].wait()
    for j in range(1, owners):
        support_copy(j).start()
    for j in range(1, owners):
        ask_copy(j).wait_recv()
    move = pltpu.make_async_copy(asked_vmem, asked_smem, load_sems.at[5])
    move.start()
    move.wait()

    def asked(r, j):
        return asked_smem[r, 0, j]

    def same(r, q, j):
        return jnp.where(asked(r, j) == asked(q, j), 1.0, 0.0).astype(F32)

    loads[2].wait()
    codes_now = codes_ref[...].astype(F32).T
    master[...] = codes_now
    codes_all[me] = codes_now.astype(BF16)
    for k in range(1, group):
        codes_copy(k).start()
    for h in range(1, groups):
        far_copy(h).start()

    loads[3].wait()

    def send_panels(a, _):
        def gather(h, _):
            region = h * group + a
            for k in range(group):
                staged[k, region] = pool[asked(region, me), :, k * width:(k + 1) * width]
            return 0

        lax.fori_loop(0, groups, gather, 0)
        for j in range(1, owners):
            panel_copy(a, j).start()
        panels[a, me] = staged[spot, base + a]
        return 0

    lax.fori_loop(0, group, send_panels, 0)

    loads[4].wait()
    for k in range(1, group):
        pixel_copy(k).start()
    pixels[spot] = patterns_ref[:, columns(spot)]

    def choose(b, _):
        place = b
        for r in range(owners):
            place = jnp.where(asked(r, me) == b, owned + r, place)
        chosen[b] = place
        return 0

    lax.fori_loop(0, owned, choose, 0)
    for j in range(1, owners):
        support_copy(j).wait_recv()

    def spread(target, codes_t, support_t):
        pieces = [
            codes_t[s * block_width:(s + 1) * block_width, :].astype(F32)
            for s in range(support_count)
        ]
        for m in range(owners):
            total = jnp.zeros((block_width, pattern_rows), F32)
            for s in range(support_count):
                total = jnp.where(support_t[s:s + 1, :] == m, pieces[s], total)
            target[m * block_width:(m + 1) * block_width, :] = total.astype(BF16)

    def pick(step, a, support_t):
        for s in range(support_count):
            total = jnp.zeros((block_width, pattern_rows), F32)
            for m in range(owners):
                total = jnp.where(
                    support_t[s:s + 1, :] == m,
                    products[m * block_width:(m + 1) * block_width, :], total,
                )
            part_out[step, a, s * block_width:(s + 1) * block_width, :] = (
                scale_factor * total
            ).astype(BF16)

    def first(a, _):
        region = base + a
        k = lax.rem(spot - a + group, group)

        @pl.when(k > 0)
        def _():
            codes_copy(k).wait_recv()
            pixel_copy(k).wait_recv()

        support_t = support_all[region]
        spread(dense.at[a], codes_all[region], support_t)
        for j in range(1, owners):
            panel_copy(a, j).wait_recv()
        panel = panels[a].reshape(owners * block_width, width)
        coefficients = dense[a]
        rebuilt = scale_factor * lax.dot_general(
            coefficients, panel, FIRST_TO_FIRST, preferred_element_type=F32
        )
        residual = (pixels[a].astype(F32) - rebuilt).astype(BF16)
        residuals[region] = residual
        for h in range(1, groups):
            residual_copy(a, h).start()
        products[...] = lax.dot_general(panel, residual, LAST_TO_LAST, preferred_element_type=F32)
        pick(0, a, support_t)

        @pl.when(k > 0)
        def _():
            part_copy(0, lax.rem(a - spot + group, group)).start()

        terms[a] = scale_factor * jnp.dot(coefficients, residual, preferred_element_type=F32)
        return 0

    lax.fori_loop(0, group, first, 0)

    for h in range(1, groups):
        far_copy(h).wait_recv()
        for k in range(1, group):
            fan_copy(h, k).start()

    def own_sums(a, _):
        def slot(j, _):
            rows = pl.ds(pl.multiple_of(j * block_width, block_width), block_width)
            total = jnp.zeros((block_width, width), F32)
            for q in range(group):
                total = total + same(base + a, base + q, j) * terms[q, rows]
            sums[a, rows] = total
            return 0

        return lax.fori_loop(0, owners, slot, 0)

    lax.fori_loop(0, group, own_sums, 0)

    for h in range(1, groups):
        for k in range(1, group):
            fan_copy(h, k).wait_recv()
        for j in range(1, row_count):
            lift_copy(h, j).start()

    def reduce_codes(step):
        total = part_out[step, spot].astype(F32)
        for k in range(1, group):
            part_copy(step, k).wait_recv()
            total = total + part_in[step, lax.rem(spot + group - k, group)].astype(F32)
        row_parts[step, my_row] = total.astype(BF16)
        for j in range(1, row_count):
            row_copy(step, j).start()

    def finish_codes(step):
        for j in range(1, row_count):
            row_copy(step, j).wait_recv()
        total = row_parts[step, 0].astype(F32)
        for i in range(1, row_count):
            total = total + row_parts[step, i].astype(F32)
        master[...] += CODE_RATE * total

    reduce_codes(0)
    for h in range(1, groups):
        for j in range(1, row_count):
            lift_copy(h, j).wait_recv()
    finish_codes(0)
    codes_next[spot] = master[...].astype(BF16)
    for k in range(1, group):
        next_copy(k).start()

    def far_sums(a, _):
        def from_group(h, _):
            q = other(h) * group + a
            spread(spare, codes_all[q], support_all[q])
            residual_copy(a, h).wait_recv()
            far_terms[...] = scale_factor * jnp.dot(
                spare[...], residuals[q], preferred_element_type=F32
            )

            def slot(j, _):
                rows = pl.ds(pl.multiple_of(j * block_width, block_width), block_width)
                term = far_terms[rows]
                for r in range(group):
                    sums[r, rows] += same(base + r, q, j) * term
                return 0

            return lax.fori_loop(0, owners, slot, 0)

        return lax.fori_loop(1, groups, from_group, 0)

    lax.fori_loop(0, group, far_sums, 0)
    for k in range(1, group):
        next_copy(k).wait_recv()

    def second(a, _):
        region = base + a
        spread(dense.at[a], codes_next[a], support_all[region])
        panel = (
            panels[a].reshape(owners * block_width, width).astype(F32) + ATOM_RATE * sums[a]
        ).astype(BF16)
        panels_next[a] = panel
        coefficients = dense[a]
        rebuilt = scale_factor * lax.dot_general(
            coefficients, panel, FIRST_TO_FIRST, preferred_element_type=F32
        )
        residual = (pixels[a].astype(F32) - rebuilt).astype(BF16)
        residuals_next[a] = residual
        after = terms[a] + scale_factor * jnp.dot(
            coefficients, residual, preferred_element_type=F32
        )
        term_out[a] = after.astype(BF16).reshape(owners, block_width, width)
        for j in range(1, owners):
            term_copy(a, j).start()
        arrived[region, spot] = term_out[a, me]
        return 0

    lax.fori_loop(0, group, second, 0)

    def third(a, _):
        products[...] = lax.dot_general(
            panels_next[a], residuals_next[a], LAST_TO_LAST, preferred_element_type=F32
        )
        pick(1, a, support_all[base + a])

        @pl.when(a != spot)
        def _():
            part_copy(1, lax.rem(a - spot + group, group)).start()

        return 0

    lax.fori_loop(0, group, third, 0)
    reduce_codes(1)
    finish_codes(1)
    codes_out[...] = master[...].T

    def gather_terms(a, _):
        for j in range(1, owners):
            term_copy(a, j).wait_recv()

        def one_slot(r, _):
            for k in range(group):
                total = totals[r, k]
                for h in range(groups):
                    q = h * group + a
                    total = total + same(r, q, me) * arrived[q, k].astype(F32)
                totals[r, k] = total
            return 0

        return lax.fori_loop(0, owners, one_slot, 0)

    totals[...] = jnp.zeros_like(totals)
    lax.fori_loop(0, group, gather_terms, 0)

    def new_block(r, _):
        for k in range(group):
            pool[owned + r, :, k * width:(k + 1) * width] = (
                staged[k, r].astype(F32) + ATOM_RATE * totals[r, k]
            ).astype(BF16)
        return 0

    lax.fori_loop(0, owners, new_block, 0)

    def place_block(b, _):
        dictionary_out[b] = pool[chosen[b]]
        return 0

    lax.fori_loop(0, owned, place_block, 0)

    def drain(a, _):
        for j in range(1, owners):
            panel_copy(a, j).wait_send()
            term_copy(a, j).wait_send()
        for h in range(1, groups):
            residual_copy(a, h).wait_send()
        return 0

    lax.fori_loop(0, group, drain, 0)
    for j in range(1, owners):
        ask_copy(j).wait_send()
        support_copy(j).wait_send()
    for k in range(1, group):
        codes_copy(k).wait_send()
        pixel_copy(k).wait_send()
        next_copy(k).wait_send()
        for step in range(2):
            part_copy(step, k).wait_send()
    for j in range(1, row_count):
        for step in range(2):
            row_copy(step, j).wait_send()
    for h in range(1, groups):
        far_copy(h).wait_send()
        for k in range(1, group):
            fan_copy(h, k).wait_send()
        for j in range(1, row_count):
            lift_copy(h, j).wait_send()


def group_size(owners, pixel_count):
    group = owners // 2
    while group > 1 and (owners % group or pixel_count % (group * LANES)):
        group //= 2
    return group


def local(patterns, dictionary, codes, support, wanted):
    owners = lax.axis_size("blk")
    row_count = lax.axis_size("rows")
    pattern_rows, pixel_count = patterns.shape
    support_count = support.shape[1]
    code_width = codes.shape[1]
    block_width = code_width // support_count
    owned = dictionary.shape[0] // block_width
    scale_factor = code_width ** (-0.5)
    group = group_size(owners, pixel_count)
    groups = owners // group
    width = pixel_count // group
    atoms = owners * block_width
    blocks = dictionary.reshape(owned, block_width, pixel_count)
    vmem = pl.BlockSpec(memory_space=pltpu.VMEM)
    hbm = pl.BlockSpec(memory_space=pltpu.HBM)
    dma = pltpu.SemaphoreType.DMA
    dictionary_after, codes_after = pl.pallas_call(
        functools.partial(steps_kernel, owners, row_count, group, block_width, scale_factor),
        out_shape=(
            jax.ShapeDtypeStruct((owned, block_width, pixel_count), BF16),
            jax.ShapeDtypeStruct((pattern_rows, code_width), F32),
        ),
        in_specs=[hbm] * 5,
        out_specs=(vmem, vmem),
        scratch_shapes=[
            pltpu.VMEM((owned + owners, block_width, pixel_count), BF16),
            pltpu.VMEM(patterns.shape, BF16),
            pltpu.VMEM(codes.shape, BF16),
            pltpu.VMEM((owners,) + support.shape[::-1], jnp.int32),
            pltpu.VMEM((owners,) + wanted.shape, jnp.int32),
            pltpu.SMEM((owners,) + wanted.shape, jnp.int32),
            pltpu.SMEM((owned,), jnp.int32),
            pltpu.VMEM((owners, code_width, pattern_rows), BF16),
            pltpu.VMEM((group, owners, block_width, width), BF16),
            pltpu.VMEM((group, owners, block_width, width), BF16),
            pltpu.VMEM((group, pattern_rows, width), BF16),
            pltpu.VMEM((group, atoms, pattern_rows), BF16),
            pltpu.VMEM((atoms, pattern_rows), BF16),
            pltpu.VMEM((owners, pattern_rows, width), BF16),
            pltpu.VMEM((group, atoms, width), F32),
            pltpu.VMEM((group, atoms, width), F32),
            pltpu.VMEM((atoms, pattern_rows), F32),
            pltpu.VMEM((atoms, width), F32),
            pltpu.VMEM((group, atoms, width), BF16),
            pltpu.VMEM((group, pattern_rows, width), BF16),
            pltpu.VMEM((group, owners, block_width, width), BF16),
            pltpu.VMEM((owners, group, block_width, width), BF16),
            pltpu.VMEM((owners, group, block_width, width), F32),
            pltpu.VMEM((2, group, code_width, pattern_rows), BF16),
            pltpu.VMEM((2, group, code_width, pattern_rows), BF16),
            pltpu.VMEM((2, row_count, code_width, pattern_rows), BF16),
            pltpu.VMEM((code_width, pattern_rows), F32),
            pltpu.VMEM((group, code_width, pattern_rows), BF16),
            dma((6,)),
            dma((owners,)), dma((owners,)),
            dma((owners,)), dma((owners,)),
            dma((group,)), dma((group,)),
            dma((groups,)), dma((groups,)),
            dma((groups, group)), dma((groups, group)),
            dma((groups, row_count)), dma((groups, row_count)),
            dma((group,)), dma((group,)),
            dma((group, owners)), dma((group, owners)),
            dma((group, groups)), dma((group, groups)),
            dma((2, group)), dma((2, group)),
            dma((2, row_count)), dma((2, row_count)),
            dma((group,)), dma((group,)),
            dma((group, owners)), dma((group, owners)),
        ],
        compiler_params=pltpu.CompilerParams(
            collective_id=0, has_side_effects=True, vmem_limit_bytes=60 * 1024 * 1024
        ),
    )(wanted, support.T, codes, patterns, blocks)
    return (dictionary_after.reshape(dictionary.shape), codes_after)


def solution(mesh):
    placed = (P("blk", "rows"), P("blk", "rows"), P("blk", None), P("blk", None), P("blk", None))
    return jax.shard_map(
        local,
        mesh=mesh,
        in_specs=placed,
        out_specs=(P("blk", "rows"), P("blk", None)),
        check_vma=False,
    )
```

```python
import functools

import jax
import jax.numpy as jnp
from jax import lax
from jax.experimental import pallas as pl
from jax.experimental.pallas import tpu as pltpu
from jax.sharding import PartitionSpec as P

CODE_RATE = 0.05
ATOM_RATE = 0.2
LANES = 128
WINDOW = 2
TERMS_WINDOW = 2
MESH = pl.DeviceIdType.MESH
F32 = jnp.float32
BF16 = jnp.bfloat16
FIRST_TO_FIRST = (((0,), (0,)), ((), ()))
LAST_TO_LAST = (((1,), (1,)), ((), ()))


def steps_kernel(
    owners, row_count, group, pieces, block_width, scale_factor,
    wanted_hbm, support_hbm, codes_hbm, patterns_hbm, dictionary_hbm,
    dictionary_out, codes_out,
    pool, patterns_ref, codes_ref, support_all, asked_vmem, asked_smem, chosen,
    codes_all, staged, panels, pixels, dense, dense_far, residuals, terms, sums, products,
    far_terms, panels_next, residuals_next, term_out, arrived,
    part_out, twin_in, half_sums, part_in, master, codes_next,
    load_sems, ask_send, ask_recv, support_send, support_recv,
    codes_send, codes_recv, near_send, near_recv, far_send, far_recv, fan_send, fan_recv,
    lift_send, lift_recv, pixel_send, pixel_recv, panel_send, panel_recv,
    residual_send, residual_recv, twin_send, twin_recv, part_send, part_recv,
    row_send, row_recv, next_send, next_recv, mate_send, mate_recv, term_send, term_recv,
):
    me = lax.axis_index("blk")
    my_row = lax.axis_index("rows")
    groups = owners // group
    mine = me // group
    spot = lax.rem(me, group)
    base = mine * group
    owned = dictionary_out.shape[0]
    pattern_rows, pixel_count = patterns_ref.shape
    support_count = support_hbm.shape[0]
    code_width = codes_ref.shape[1]
    width = pixel_count // group
    piece_width = width // pieces
    share = code_width // 2
    core = lax.rem(my_row, 2)
    pair = my_row // 2
    pairs = row_count // 2
    twin = {"rows": pair * 2 + 1 - core}
    kept = pl.ds(pl.multiple_of(core * share, share), share)
    given = pl.ds(pl.multiple_of((1 - core) * share, share), share)
    quarter = share // pairs
    mine_rows = pl.ds(pl.multiple_of(core * share + pair * quarter, quarter), quarter)
    sharers = [(k, m) for m in range(pairs) for k in range(group) if k or m]
    window = min(WINDOW, group)
    terms_window = min(TERMS_WINDOW, group)
    order = sorted(range(1, owners), key=lambda j: abs(2 * j - owners))

    def columns(k):
        return pl.ds(pl.multiple_of(k * width, width), width)

    loads = (
        pltpu.make_async_copy(wanted_hbm, asked_vmem.at[me], load_sems.at[0]),
        pltpu.make_async_copy(support_hbm, support_all.at[me], load_sems.at[1]),
        pltpu.make_async_copy(codes_hbm, codes_ref, load_sems.at[2]),
        pltpu.make_async_copy(dictionary_hbm, pool.at[pl.ds(0, owned)], load_sems.at[3]),
        pltpu.make_async_copy(patterns_hbm, patterns_ref, load_sems.at[4]),
    )
    for load in loads:
        load.start()

    barrier = pltpu.get_barrier_semaphore()
    for j in range(1, owners):
        pl.semaphore_signal(
            barrier, inc=1, device_id={"blk": lax.rem(me + j, owners)}, device_id_type=MESH
        )
    for j in range(1, row_count):
        pl.semaphore_signal(
            barrier, inc=1, device_id={"rows": lax.rem(my_row + j, row_count)}, device_id_type=MESH
        )
    for k in range(1, group):
        for m in range(1, pairs):
            pl.semaphore_signal(
                barrier, inc=1,
                device_id={"blk": base + lax.rem(spot + k, group),
                           "rows": lax.rem(my_row + 2 * m, row_count)},
                device_id_type=MESH,
            )
    pl.semaphore_wait(barrier, owners + row_count - 2 + (group - 1) * (pairs - 1))

    def remote(source, target, send, recv, device):
        return pltpu.make_async_remote_copy(
            src_ref=source, dst_ref=target, send_sem=send, recv_sem=recv,
            device_id=device, device_id_type=MESH,
        )

    def peer(j):
        return lax.rem(me + j, owners)

    def beside(k):
        return lax.rem(spot + k, group)

    def other(h):
        return lax.rem(mine + h, groups)

    def row_peer(j):
        return {"rows": lax.rem(my_row + 2 * j, row_count)}

    def ask_copy(j):
        return remote(asked_vmem.at[me], asked_vmem.at[me], ask_send.at[j], ask_recv.at[j],
                      {"blk": peer(j)})

    def support_copy(j):
        return remote(support_all.at[me], support_all.at[me], support_send.at[j],
                      support_recv.at[j], {"blk": peer(j)})

    def codes_copy(k):
        part = codes_all.at[me, kept]
        return remote(part, part, codes_send.at[k], codes_recv.at[k],
                      {"blk": base + beside(k)})

    def near_copy(k):
        part = codes_all.at[base + beside(group - k), kept]
        return remote(part, part, near_send.at[k], near_recv.at[k], twin)

    def far_copy(h):
        part = codes_all.at[me, kept]
        return remote(part, part, far_send.at[h], far_recv.at[h],
                      {"blk": other(h) * group + spot})

    def fan_copy(h, k):
        part = codes_all.at[other(groups - h) * group + spot, kept]
        return remote(part, part, fan_send.at[h, k], fan_recv.at[h, k],
                      {"blk": base + beside(k)})

    def lift_copy(h):
        part = codes_all.at[pl.ds(other(h) * group, group), kept]
        return remote(part, part, lift_send.at[h], lift_recv.at[h], twin)

    def pixel_copy(k):
        return remote(patterns_ref.at[:, columns(beside(k))], pixels.at[spot],
                      pixel_send.at[k], pixel_recv.at[k], {"blk": base + beside(k)})

    def panel_copy(a, j):
        to = peer(j)
        return remote(staged.at[lax.rem(to, group), (to // group) * group + a],
                      panels.at[a, me], panel_send.at[a, j], panel_recv.at[a, j], {"blk": to})

    def residual_copy(a, h, i):
        part = residuals.at[base + a, i]
        return remote(part, part, residual_send.at[a, h, i], residual_recv.at[a, h, i],
                      {"blk": other(h) * group + spot})

    def twin_copy(step, a):
        return remote(part_out.at[step, a, given], twin_in.at[step, a],
                      twin_send.at[step, a], twin_recv.at[step, a], twin)

    def sharer(k, m):
        return {"blk": base + beside(k), "rows": lax.rem(my_row + 2 * m, row_count)}

    def part_copy(step, k, m):
        to = lax.rem(pair + m, pairs)
        rows = pl.ds(pl.multiple_of(to * quarter, quarter), quarter)
        return remote(half_sums.at[step, beside(k), rows], part_in.at[step, spot, pair],
                      part_send.at[step, k, m], part_recv.at[step, k, m], sharer(k, m))

    def next_copy(k, m):
        part = codes_next.at[spot, mine_rows]
        return remote(part, part, next_send.at[k, m], next_recv.at[k, m], sharer(k, m))

    def row_copy(j):
        part = master.at[mine_rows]
        return remote(part, part, row_send.at[j], row_recv.at[j], row_peer(j))

    def mate_copy():
        part = codes_next.at[:, kept]
        return remote(part, part, mate_send.at[0], mate_recv.at[0], twin)

    def last_copy():
        part = master.at[kept]
        return remote(part, part, mate_send.at[1], mate_recv.at[1], twin)

    def term_copy(a, j, i):
        to = peer(j)
        return remote(term_out.at[a, i, to], arrived.at[base + a, spot, i],
                      term_send.at[a, j, i], term_recv.at[a, j, i], {"blk": to})

    loads[0].wait()
    for j in order:
        ask_copy(j).start()
    loads[2].wait()
    codes_now = codes_ref[...].astype(F32).T
    master[...] = codes_now
    codes_all[me] = codes_now.astype(BF16)
    for h in range(1, groups):
        far_copy(h).start()
    for k in range(1, group):
        codes_copy(k).start()
    loads[1].wait()
    for j in order:
        support_copy(j).start()
    loads[4].wait()
    for k in range(1, group):
        pixel_copy(k).start()
    pixels[spot] = patterns_ref[:, columns(spot)]

    for j in order:
        ask_copy(j).wait_recv()
    move = pltpu.make_async_copy(asked_vmem, asked_smem, load_sems.at[5])
    move.start()
    move.wait()

    def asked(r, j):
        return asked_smem[r, 0, j]

    def same(r, q, j):
        return jnp.where(asked(r, j) == asked(q, j), 1.0, 0.0).astype(F32)

    loads[3].wait()

    def gather_panels(a):
        def gather(h, _):
            region = h * group + a
            for k in range(group):
                staged[k, region] = pool[asked(region, me), :, k * width:(k + 1) * width]
            return 0

        lax.fori_loop(0, groups, gather, 0)
        panels[a, me] = staged[spot, base + a]

    gather_panels(0)
    for j in order:
        panel_copy(0, j).start()

    def gather_more(a, _):
        gather_panels(a)
        return 0

    lax.fori_loop(1, group, gather_more, 0)

    def choose(b, _):
        place = b
        for r in range(owners):
            place = jnp.where(asked(r, me) == b, owned + r, place)
        chosen[b] = place
        return 0

    lax.fori_loop(0, owned, choose, 0)
    for k in range(1, group):
        codes_copy(k).wait_recv()
        near_copy(k).start()
    for j in range(1, owners):
        support_copy(j).wait_recv()

    def spread(target, codes_t, support_t):
        given_codes = [
            codes_t[s * block_width:(s + 1) * block_width, :].astype(F32)
            for s in range(support_count)
        ]
        for m in range(owners):
            total = jnp.zeros((block_width, pattern_rows), F32)
            for s in range(support_count):
                total = jnp.where(support_t[s:s + 1, :] == m, given_codes[s], total)
            target[m * block_width:(m + 1) * block_width, :] = total.astype(BF16)

    def pick(step, a, support_t):
        for s in range(support_count):
            total = jnp.zeros((block_width, pattern_rows), F32)
            for m in range(owners):
                total = jnp.where(
                    support_t[s:s + 1, :] == m,
                    products[m * block_width:(m + 1) * block_width, :], total,
                )
            part_out[step, a, s * block_width:(s + 1) * block_width, :] = (
                scale_factor * total
            ).astype(BF16)

    def forward(step, a):
        twin_copy(step, a).wait_recv()
        half_sums[step, a] = (
            part_out[step, a, kept].astype(F32) + twin_in[step, a].astype(F32)
        ).astype(BF16)

        k = lax.rem(a - spot + group, group)
        for m in range(1, pairs):
            part_copy(step, k, m).start()

        @pl.when(k > 0)
        def _():
            part_copy(step, k, 0).start()

        @pl.when(k == 0)
        def _():
            rows = pl.ds(pl.multiple_of(pair * quarter, quarter), quarter)
            part_in[step, spot, pair] = half_sums[step, spot, rows]

    def first(a, _):
        region = base + a
        k = lax.rem(spot - a + group, group)

        @pl.when(a + 1 < group)
        def _():
            for j in order:
                panel_copy(a, j).wait_send()
                panel_copy(a + 1, j).start()

        @pl.when(k > 0)
        def _():
            near_copy(k).wait_recv()

        support_t = support_all[region]
        spread(dense.at[a], codes_all[region], support_t)

        @pl.when(k > 0)
        def _():
            pixel_copy(k).wait_recv()

        for j in range(1, owners):
            panel_copy(a, j).wait_recv()
        panel = panels[a].reshape(owners * block_width, width)
        coefficients = dense[a]
        rebuilt = scale_factor * lax.dot_general(
            coefficients, panel, FIRST_TO_FIRST, preferred_element_type=F32
        )
        residual = (pixels[a].astype(F32) - rebuilt).astype(BF16)
        for i in range(pieces):
            residuals[region, i] = residual[:, i * piece_width:(i + 1) * piece_width]

        @pl.when(a < window)
        def _():
            for h in range(1, groups):
                residual_copy(a, h, 0).start()

        products[...] = lax.dot_general(panel, residual, LAST_TO_LAST, preferred_element_type=F32)
        pick(0, a, support_t)
        twin_copy(0, a).start()
        terms[a] = scale_factor * jnp.dot(coefficients, residual, preferred_element_type=F32)

        @pl.when(a > 0)
        def _():
            forward(0, a - 1)

        @pl.when(a == 0)
        def _():
            for h in range(1, groups):
                far_copy(h).wait_recv()
                for k in range(1, group):
                    fan_copy(h, k).start()

        @pl.when(a == group - 1)
        def _():
            for h in range(1, groups):
                for k in range(1, group):
                    fan_copy(h, k).wait_recv()
            for h in range(1, groups):
                lift_copy(h).start()

        return 0

    lax.fori_loop(0, group, first, 0)
    queue = [(a, i) for i in range(pieces) for a in range(group)]
    waiting = queue[window:]
    sent = []

    def feed(count):
        for _ in range(count):
            if waiting:
                behind = queue[len(sent)]
                sent.append(behind)
                ahead = waiting.pop(0)
                for h in range(1, groups):
                    residual_copy(behind[0], h, behind[1]).wait_send()
                    residual_copy(ahead[0], h, ahead[1]).start()

    forward(0, group - 1)
    feed(1)

    def own_sums(a, _):
        def slot(j, _):
            rows = pl.ds(pl.multiple_of(j * block_width, block_width), block_width)
            total = jnp.zeros((block_width, width), F32)
            for q in range(group):
                total = total + same(base + a, base + q, j) * terms[q, rows]
            sums[a, rows] = total
            return 0

        return lax.fori_loop(0, owners, slot, 0)

    lax.fori_loop(0, group, own_sums, 0)
    feed(1)

    def reduce_codes(step):
        for k, m in sharers:
            part_copy(step, k, m).wait_recv()
        total = jnp.zeros((quarter, pattern_rows), F32)
        for k in range(group):
            for m in range(pairs):
                total = total + part_in[step, k, m].astype(F32)
        master[mine_rows] += CODE_RATE * total

    reduce_codes(0)
    codes_next[spot, mine_rows] = master[mine_rows].astype(BF16)
    for k, m in sharers:
        next_copy(k, m).start()
    feed(2)
    for h in range(1, groups):
        lift_copy(h).wait_recv()

    def spread_far(a, _):
        def from_group(h, _):
            q = other(h) * group + a
            spread(dense_far.at[(h - 1) * group + a], codes_all[q], support_all[q])
            return 0

        return lax.fori_loop(1, groups, from_group, 0)

    if pieces > 1:
        lax.fori_loop(0, group, spread_far, 0)
    for k, m in sharers:
        next_copy(k, m).wait_recv()
    mate_copy().start()
    feed(len(waiting))

    def far_sums(i):
        lanes = slice(i * piece_width, (i + 1) * piece_width)

        def from_region(a, _):
            def from_group(h, _):
                q = other(groups - h) * group + a
                place = 0
                if pieces > 1:
                    place = (groups - h - 1) * group + a
                else:
                    spread(dense_far.at[0], codes_all[q], support_all[q])
                residual_copy(a, h, i).wait_recv()
                far_terms[...] = scale_factor * jnp.dot(
                    dense_far[place], residuals[q, i], preferred_element_type=F32
                )

                def slot(j, _):
                    rows = pl.ds(pl.multiple_of(j * block_width, block_width), block_width)
                    term = far_terms[rows]
                    for r in range(group):
                        sums[r, rows, lanes] += same(base + r, q, j) * term
                    return 0

                return lax.fori_loop(0, owners, slot, 0)

            return lax.fori_loop(1, groups, from_group, 0)

        lax.fori_loop(0, group, from_region, 0)

    def second(i):
        lanes = slice(i * piece_width, (i + 1) * piece_width)

        def region_work(a, _):
            region = base + a
            panel = (
                panels[a, :, :, lanes].reshape(owners * block_width, piece_width).astype(F32)
                + ATOM_RATE * sums[a, :, lanes]
            ).astype(BF16)
            panels_next[a, :, lanes] = panel
            coefficients = dense[a]
            rebuilt = scale_factor * lax.dot_general(
                coefficients, panel, FIRST_TO_FIRST, preferred_element_type=F32
            )
            residual = (pixels[a, :, lanes].astype(F32) - rebuilt).astype(BF16)
            residuals_next[a, :, lanes] = residual
            after = terms[a, :, lanes] + scale_factor * jnp.dot(
                coefficients, residual, preferred_element_type=F32
            )
            term_out[a, i] = after.astype(BF16).reshape(owners, block_width, piece_width)

            @pl.when(a < terms_window)
            def _():
                for j in order:
                    term_copy(a, j, i).start()

            arrived[region, spot, i] = term_out[a, i, me]
            return 0

        lax.fori_loop(0, group, region_work, 0)

    def feed_terms(a, i):
        if terms_window <= a < group:
            for j in order:
                term_copy(a - terms_window, j, i).wait_send()
                term_copy(a, j, i).start()

    def spread_next(a, _):
        spread(dense.at[a], codes_next[a], support_all[base + a])
        return 0

    far_sums(0)
    mate_copy().wait_recv()
    lax.fori_loop(0, group, spread_next, 0)
    second(0)
    for i in range(1, pieces):
        for a in range(group):
            feed_terms(a, i - 1)
        far_sums(i)
        second(i)

    def third(a, _):
        products[...] = lax.dot_general(
            panels_next[a], residuals_next[a], LAST_TO_LAST, preferred_element_type=F32
        )
        pick(1, a, support_all[base + a])
        twin_copy(1, a).start()

        @pl.when(a > 0)
        def _():
            forward(1, a - 1)

        return 0

    lax.fori_loop(0, group, third, 0)
    forward(1, group - 1)
    feed_terms(terms_window, pieces - 1)
    reduce_codes(1)
    for j in range(1, pairs):
        row_copy(j).start()
    for a in range(terms_window + 1, group):
        feed_terms(a, pieces - 1)
    for j in range(1, pairs):
        row_copy(j).wait_recv()
    last_copy().start()

    def new_blocks(i):
        for a in range(group):
            for j in range(1, owners):
                term_copy(a, j, i).wait_recv()

        def one_slot(r, _):
            for k in range(group):
                start = k * width + i * piece_width
                total = jnp.zeros((block_width, piece_width), F32)
                for q in range(owners):
                    total = total + same(r, q, me) * arrived[q, k, i].astype(F32)
                before = staged[k, r, :, i * piece_width:(i + 1) * piece_width]
                pool[owned + r, :, start:start + piece_width] = (
                    before.astype(F32) + ATOM_RATE * total
                ).astype(BF16)
            return 0

        lax.fori_loop(0, owners, one_slot, 0)

    new_blocks(0)
    last_copy().wait_recv()
    codes_out[...] = master[...].T
    for i in range(1, pieces):
        new_blocks(i)

    def place_block(b, _):
        dictionary_out[b] = pool[chosen[b]]
        return 0

    lax.fori_loop(0, owned, place_block, 0)

    def drain(a, _):
        for step in range(2):
            twin_copy(step, a).wait_send()
        return 0

    lax.fori_loop(0, group, drain, 0)
    for a, i in queue[len(sent):]:
        for h in range(1, groups):
            residual_copy(a, h, i).wait_send()
    for a in range(group):
        for i in range(pieces):
            if a + terms_window >= group:
                for j in order:
                    term_copy(a, j, i).wait_send()
    for j in range(1, owners):
        panel_copy(group - 1, j).wait_send()
        ask_copy(j).wait_send()
        support_copy(j).wait_send()
    for k in range(1, group):
        codes_copy(k).wait_send()
        near_copy(k).wait_send()
        pixel_copy(k).wait_send()
    for k, m in sharers:
        next_copy(k, m).wait_send()
        for step in range(2):
            part_copy(step, k, m).wait_send()
    for j in range(1, pairs):
        row_copy(j).wait_send()
    for h in range(1, groups):
        far_copy(h).wait_send()
        for k in range(1, group):
            fan_copy(h, k).wait_send()
        lift_copy(h).wait_send()
    mate_copy().wait_send()
    last_copy().wait_send()


def group_size(owners, pixel_count):
    group = owners // 2
    while group > 1 and (owners % group or pixel_count % (group * LANES)):
        group //= 2
    return group


def local(patterns, dictionary, codes, support, wanted):
    owners = lax.axis_size("blk")
    row_count = lax.axis_size("rows")
    pattern_rows, pixel_count = patterns.shape
    support_count = support.shape[1]
    code_width = codes.shape[1]
    block_width = code_width // support_count
    owned = dictionary.shape[0] // block_width
    scale_factor = code_width ** (-0.5)
    group = group_size(owners, pixel_count)
    groups = owners // group
    width = pixel_count // group
    pieces = 2 if width % (2 * LANES) == 0 else 1
    piece_width = width // pieces
    share = code_width // 2
    pairs = row_count // 2
    atoms = owners * block_width
    blocks = dictionary.reshape(owned, block_width, pixel_count)
    vmem = pl.BlockSpec(memory_space=pltpu.VMEM)
    hbm = pl.BlockSpec(memory_space=pltpu.HBM)
    dma = pltpu.SemaphoreType.DMA
    dictionary_after, codes_after = pl.pallas_call(
        functools.partial(steps_kernel, owners, row_count, group, pieces, block_width, scale_factor),
        out_shape=(
            jax.ShapeDtypeStruct((owned, block_width, pixel_count), BF16),
            jax.ShapeDtypeStruct((pattern_rows, code_width), F32),
        ),
        in_specs=[hbm] * 5,
        out_specs=(vmem, vmem),
        scratch_shapes=[
            pltpu.VMEM((owned + owners, block_width, pixel_count), BF16),
            pltpu.VMEM(patterns.shape, BF16),
            pltpu.VMEM(codes.shape, BF16),
            pltpu.VMEM((owners,) + support.shape[::-1], jnp.int32),
            pltpu.VMEM((owners,) + wanted.shape, jnp.int32),
            pltpu.SMEM((owners,) + wanted.shape, jnp.int32),
            pltpu.SMEM((owned,), jnp.int32),
            pltpu.VMEM((owners, code_width, pattern_rows), BF16),
            pltpu.VMEM((group, owners, block_width, width), BF16),
            pltpu.VMEM((group, owners, block_width, width), BF16),
            pltpu.VMEM((group, pattern_rows, width), BF16),
            pltpu.VMEM((group, atoms, pattern_rows), BF16),
            pltpu.VMEM((owners - group if pieces > 1 else 1, atoms, pattern_rows), BF16),
            pltpu.VMEM((owners, pieces, pattern_rows, piece_width), BF16),
            pltpu.VMEM((group, atoms, width), F32),
            pltpu.VMEM((group, atoms, width), F32),
            pltpu.VMEM((atoms, pattern_rows), F32),
            pltpu.VMEM((atoms, piece_width), F32),
            pltpu.VMEM((group, atoms, width), BF16),
            pltpu.VMEM((group, pattern_rows, width), BF16),
            pltpu.VMEM((group, pieces, owners, block_width, piece_width), BF16),
            pltpu.VMEM((owners, group, pieces, block_width, piece_width), BF16),
            pltpu.VMEM((2, group, code_width, pattern_rows), BF16),
            pltpu.VMEM((2, group, share, pattern_rows), BF16),
            pltpu.VMEM((2, group, share, pattern_rows), BF16),
            pltpu.VMEM((2, group, pairs, share // pairs, pattern_rows), BF16),
            pltpu.VMEM((code_width, pattern_rows), F32),
            pltpu.VMEM((group, code_width, pattern_rows), BF16),
            dma((6,)),
            dma((owners,)), dma((owners,)),
            dma((owners,)), dma((owners,)),
            dma((group,)), dma((group,)),
            dma((group,)), dma((group,)),
            dma((groups,)), dma((groups,)),
            dma((groups, group)), dma((groups, group)),
            dma((groups,)), dma((groups,)),
            dma((group,)), dma((group,)),
            dma((group, owners)), dma((group, owners)),
            dma((group, groups, pieces)), dma((group, groups, pieces)),
            dma((2, group)), dma((2, group)),
            dma((2, group, pairs)), dma((2, group, pairs)),
            dma((pairs,)), dma((pairs,)),
            dma((group, pairs)), dma((group, pairs)),
            dma((2,)), dma((2,)),
            dma((group, owners, pieces)), dma((group, owners, pieces)),
        ],
        compiler_params=pltpu.CompilerParams(
            collective_id=0, has_side_effects=True, vmem_limit_bytes=49 * 1024 * 1024
        ),
    )(wanted, support.T, codes, patterns, blocks)
    return (dictionary_after.reshape(dictionary.shape), codes_after)


def solution(mesh):
    placed = (P("blk", "rows"), P("blk", "rows"), P("blk", None), P("blk", None), P("blk", None))
    return jax.shard_map(
        local,
        mesh=mesh,
        in_specs=placed,
        out_specs=(P("blk", "rows"), P("blk", None)),
        check_vma=False,
    )
```

```python
import functools

import jax
import jax.numpy as jnp
from jax import lax
from jax.experimental import pallas as pl
from jax.experimental.pallas import tpu as pltpu
from jax.sharding import PartitionSpec as P

CODE_RATE = 0.05
ATOM_RATE = 0.2
LANES = 128
WINDOW = 3
TERMS_WINDOW = 2
MESH = pl.DeviceIdType.MESH
F32 = jnp.float32
BF16 = jnp.bfloat16
FIRST_TO_FIRST = (((0,), (0,)), ((), ()))
LAST_TO_LAST = (((1,), (1,)), ((), ()))


def steps_kernel(
    owners, row_count, group, pieces, block_width, scale_factor,
    wanted_hbm, support_hbm, codes_hbm, patterns_hbm, dictionary_hbm,
    dictionary_out, codes_out,
    pool, patterns_ref, codes_ref, support_all, asked_vmem, asked_smem, chosen,
    codes_all, staged, panels, pixels, dense, dense_far, residuals, terms, sums, products,
    far_terms, panels_next, residuals_next, term_out, arrived,
    part_out, twin_in, half_sums, part_in, master, codes_next,
    load_sems, ask_send, ask_recv, support_send, support_recv,
    codes_send, codes_recv, near_send, near_recv, far_send, far_recv, fan_send, fan_recv,
    lift_send, lift_recv, pixel_send, pixel_recv, panel_send, panel_recv,
    residual_send, residual_recv, twin_send, twin_recv, part_send, part_recv,
    row_send, row_recv, next_send, next_recv, mate_send, mate_recv, term_send, term_recv,
):
    me = lax.axis_index("blk")
    my_row = lax.axis_index("rows")
    groups = owners // group
    mine = me // group
    spot = lax.rem(me, group)
    base = mine * group
    owned = dictionary_out.shape[0]
    pattern_rows, pixel_count = patterns_ref.shape
    support_count = support_hbm.shape[0]
    code_width = codes_ref.shape[1]
    width = pixel_count // group
    piece_width = width // pieces
    share = code_width // 2
    core = lax.rem(my_row, 2)
    pair = my_row // 2
    pairs = row_count // 2
    twin = {"rows": pair * 2 + 1 - core}
    kept = pl.ds(pl.multiple_of(core * share, share), share)
    given = pl.ds(pl.multiple_of((1 - core) * share, share), share)
    quarter = share // pairs
    mine_rows = pl.ds(pl.multiple_of(core * share + pair * quarter, quarter), quarter)
    sharers = [(k, m) for m in range(pairs) for k in range(group) if k or m]
    window = min(WINDOW, group)
    terms_window = min(TERMS_WINDOW, group)
    order = sorted(range(1, owners), key=lambda j: abs(2 * j - owners))

    def columns(k):
        return pl.ds(pl.multiple_of(k * width, width), width)

    loads = (
        pltpu.make_async_copy(wanted_hbm, asked_vmem.at[me], load_sems.at[0]),
        pltpu.make_async_copy(support_hbm, support_all.at[me], load_sems.at[1]),
        pltpu.make_async_copy(codes_hbm, codes_ref, load_sems.at[2]),
        pltpu.make_async_copy(dictionary_hbm, pool.at[pl.ds(0, owned)], load_sems.at[3]),
        pltpu.make_async_copy(patterns_hbm, patterns_ref, load_sems.at[4]),
    )
    for load in loads:
        load.start()

    barrier = pltpu.get_barrier_semaphore()
    for j in range(1, owners):
        pl.semaphore_signal(
            barrier, inc=1, device_id={"blk": lax.rem(me + j, owners)}, device_id_type=MESH
        )
    for j in range(1, row_count):
        pl.semaphore_signal(
            barrier, inc=1, device_id={"rows": lax.rem(my_row + j, row_count)}, device_id_type=MESH
        )
    for k in range(1, group):
        for m in range(1, pairs):
            pl.semaphore_signal(
                barrier, inc=1,
                device_id={"blk": base + lax.rem(spot + k, group),
                           "rows": lax.rem(my_row + 2 * m, row_count)},
                device_id_type=MESH,
            )
    pl.semaphore_wait(barrier, owners + row_count - 2 + (group - 1) * (pairs - 1))

    def remote(source, target, send, recv, device):
        return pltpu.make_async_remote_copy(
            src_ref=source, dst_ref=target, send_sem=send, recv_sem=recv,
            device_id=device, device_id_type=MESH,
        )

    def peer(j):
        return lax.rem(me + j, owners)

    def beside(k):
        return lax.rem(spot + k, group)

    def other(h):
        return lax.rem(mine + h, groups)

    def row_peer(j):
        return {"rows": lax.rem(my_row + 2 * j, row_count)}

    def ask_copy(j):
        return remote(asked_vmem.at[me], asked_vmem.at[me], ask_send.at[j], ask_recv.at[j],
                      {"blk": peer(j)})

    def support_copy(j):
        return remote(support_all.at[me], support_all.at[me], support_send.at[j],
                      support_recv.at[j], {"blk": peer(j)})

    def codes_copy(k):
        part = codes_all.at[me, kept]
        return remote(part, part, codes_send.at[k], codes_recv.at[k],
                      {"blk": base + beside(k)})

    def near_copy(k):
        part = codes_all.at[base + beside(group - k), kept]
        return remote(part, part, near_send.at[k], near_recv.at[k], twin)

    def far_copy(h):
        part = codes_all.at[me, kept]
        return remote(part, part, far_send.at[h], far_recv.at[h],
                      {"blk": other(h) * group + spot})

    def fan_copy(h, k):
        part = codes_all.at[other(groups - h) * group + spot, kept]
        return remote(part, part, fan_send.at[h, k], fan_recv.at[h, k],
                      {"blk": base + beside(k)})

    def lift_copy(h):
        part = codes_all.at[pl.ds(other(h) * group, group), kept]
        return remote(part, part, lift_send.at[h], lift_recv.at[h], twin)

    def pixel_copy(k):
        return remote(patterns_ref.at[:, columns(beside(k))], pixels.at[spot],
                      pixel_send.at[k], pixel_recv.at[k], {"blk": base + beside(k)})

    def panel_copy(a, j):
        to = peer(j)
        return remote(staged.at[lax.rem(to, group), (to // group) * group + a],
                      panels.at[a, me], panel_send.at[a, j], panel_recv.at[a, j], {"blk": to})

    def residual_copy(a, h, i):
        part = residuals.at[base + a, i]
        return remote(part, part, residual_send.at[a, h, i], residual_recv.at[a, h, i],
                      {"blk": other(h) * group + spot})

    def twin_copy(step, a):
        return remote(part_out.at[step, a, given], twin_in.at[step, a],
                      twin_send.at[step, a], twin_recv.at[step, a], twin)

    def sharer(k, m):
        return {"blk": base + beside(k), "rows": lax.rem(my_row + 2 * m, row_count)}

    def part_copy(step, k, m):
        to = lax.rem(pair + m, pairs)
        rows = pl.ds(pl.multiple_of(to * quarter, quarter), quarter)
        return remote(half_sums.at[step, beside(k), rows], part_in.at[step, spot, pair],
                      part_send.at[step, k, m], part_recv.at[step, k, m], sharer(k, m))

    def next_copy(k, m):
        part = codes_next.at[spot, mine_rows]
        return remote(part, part, next_send.at[k, m], next_recv.at[k, m], sharer(k, m))

    def row_copy(j):
        part = master.at[mine_rows]
        return remote(part, part, row_send.at[j], row_recv.at[j], row_peer(j))

    def mate_copy():
        part = codes_next.at[:, kept]
        return remote(part, part, mate_send.at[0], mate_recv.at[0], twin)

    def last_copy():
        part = master.at[kept]
        return remote(part, part, mate_send.at[1], mate_recv.at[1], twin)

    def term_copy(a, j, i):
        to = peer(j)
        return remote(term_out.at[a, i, to], arrived.at[base + a, spot, i],
                      term_send.at[a, j, i], term_recv.at[a, j, i], {"blk": to})

    loads[0].wait()
    for j in order:
        ask_copy(j).start()
    loads[2].wait()
    codes_now = codes_ref[...].astype(F32).T
    master[...] = codes_now
    codes_all[me] = codes_now.astype(BF16)
    for h in range(1, groups):
        far_copy(h).start()
    for k in range(1, group):
        codes_copy(k).start()
    loads[1].wait()
    for j in order:
        support_copy(j).start()
    loads[4].wait()
    for k in range(1, group):
        pixel_copy(k).start()
    pixels[spot] = patterns_ref[:, columns(spot)]

    for j in order:
        ask_copy(j).wait_recv()
    move = pltpu.make_async_copy(asked_vmem, asked_smem, load_sems.at[5])
    move.start()
    move.wait()

    def asked(r, j):
        return asked_smem[r, 0, j]

    def same(r, q, j):
        return jnp.where(asked(r, j) == asked(q, j), 1.0, 0.0).astype(F32)

    loads[3].wait()

    def gather_panels(a):
        def gather(h, _):
            region = h * group + a
            for k in range(group):
                staged[k, region] = pool[asked(region, me), :, k * width:(k + 1) * width]
            return 0

        lax.fori_loop(0, groups, gather, 0)
        panels[a, me] = staged[spot, base + a]

    gather_panels(0)
    for j in order:
        panel_copy(0, j).start()

    def gather_more(a, _):
        gather_panels(a)
        return 0

    lax.fori_loop(1, group, gather_more, 0)

    def choose(b, _):
        place = b
        for r in range(owners):
            place = jnp.where(asked(r, me) == b, owned + r, place)
        chosen[b] = place
        return 0

    lax.fori_loop(0, owned, choose, 0)
    for k in range(1, group):
        codes_copy(k).wait_recv()
        near_copy(k).start()
    for j in range(1, owners):
        support_copy(j).wait_recv()

    def spread(target, codes_t, support_t):
        given_codes = [
            codes_t[s * block_width:(s + 1) * block_width, :].astype(F32)
            for s in range(support_count)
        ]
        for m in range(owners):
            total = jnp.zeros((block_width, pattern_rows), F32)
            for s in range(support_count):
                total = jnp.where(support_t[s:s + 1, :] == m, given_codes[s], total)
            target[m * block_width:(m + 1) * block_width, :] = total.astype(BF16)

    def pick(step, a, support_t):
        for s in range(support_count):
            total = jnp.zeros((block_width, pattern_rows), F32)
            for m in range(owners):
                total = jnp.where(
                    support_t[s:s + 1, :] == m,
                    products[m * block_width:(m + 1) * block_width, :], total,
                )
            part_out[step, a, s * block_width:(s + 1) * block_width, :] = (
                scale_factor * total
            ).astype(BF16)

    def forward(step, a):
        twin_copy(step, a).wait_recv()
        half_sums[step, a] = (
            part_out[step, a, kept].astype(F32) + twin_in[step, a].astype(F32)
        ).astype(BF16)

        k = lax.rem(a - spot + group, group)
        for m in range(1, pairs):
            part_copy(step, k, m).start()

        @pl.when(k > 0)
        def _():
            part_copy(step, k, 0).start()

        @pl.when(k == 0)
        def _():
            rows = pl.ds(pl.multiple_of(pair * quarter, quarter), quarter)
            part_in[step, spot, pair] = half_sums[step, spot, rows]

    def first(a, _):
        region = base + a
        k = lax.rem(spot - a + group, group)

        @pl.when(a + 1 < group)
        def _():
            for j in order:
                panel_copy(a, j).wait_send()
                panel_copy(a + 1, j).start()

        @pl.when(k > 0)
        def _():
            near_copy(k).wait_recv()

        support_t = support_all[region]
        spread(dense.at[a], codes_all[region], support_t)

        @pl.when(k > 0)
        def _():
            pixel_copy(k).wait_recv()

        for j in range(1, owners):
            panel_copy(a, j).wait_recv()
        panel = panels[a].reshape(owners * block_width, width)
        coefficients = dense[a]
        rebuilt = scale_factor * lax.dot_general(
            coefficients, panel, FIRST_TO_FIRST, preferred_element_type=F32
        )
        residual = (pixels[a].astype(F32) - rebuilt).astype(BF16)
        for i in range(pieces):
            residuals[region, i] = residual[:, i * piece_width:(i + 1) * piece_width]

        @pl.when(a < window)
        def _():
            for h in range(1, groups):
                residual_copy(a, h, 0).start()

        products[...] = lax.dot_general(panel, residual, LAST_TO_LAST, preferred_element_type=F32)
        pick(0, a, support_t)
        twin_copy(0, a).start()
        terms[a] = scale_factor * jnp.dot(coefficients, residual, preferred_element_type=F32)

        @pl.when(a > 0)
        def _():
            forward(0, a - 1)

        @pl.when(a == 0)
        def _():
            for h in range(1, groups):
                far_copy(h).wait_recv()
                for k in range(1, group):
                    fan_copy(h, k).start()

        @pl.when(a == group - 1)
        def _():
            for h in range(1, groups):
                for k in range(1, group):
                    fan_copy(h, k).wait_recv()
            for h in range(1, groups):
                lift_copy(h).start()

        return 0

    lax.fori_loop(0, group, first, 0)
    queue = [(a, i) for i in range(pieces) for a in range(group)]
    waiting = queue[window:]
    sent = []

    def feed(count):
        for _ in range(count):
            if waiting:
                behind = queue[len(sent)]
                sent.append(behind)
                ahead = waiting.pop(0)
                for h in range(1, groups):
                    residual_copy(behind[0], h, behind[1]).wait_send()
                    residual_copy(ahead[0], h, ahead[1]).start()

    forward(0, group - 1)
    feed(1)

    def own_sums(a, _):
        def slot(j, _):
            rows = pl.ds(pl.multiple_of(j * block_width, block_width), block_width)
            total = jnp.zeros((block_width, width), F32)
            for q in range(group):
                total = total + same(base + a, base + q, j) * terms[q, rows]
            sums[a, rows] = total
            return 0

        return lax.fori_loop(0, owners, slot, 0)

    lax.fori_loop(0, group, own_sums, 0)
    feed(1)

    def reduce_codes(step):
        for k, m in sharers:
            part_copy(step, k, m).wait_recv()
        total = jnp.zeros((quarter, pattern_rows), F32)
        for k in range(group):
            for m in range(pairs):
                total = total + part_in[step, k, m].astype(F32)
        master[mine_rows] += CODE_RATE * total

    reduce_codes(0)
    codes_next[spot, mine_rows] = master[mine_rows].astype(BF16)
    for k, m in sharers:
        next_copy(k, m).start()
    feed(2)
    for h in range(1, groups):
        lift_copy(h).wait_recv()

    def spread_far(a, _):
        def from_group(h, _):
            q = other(h) * group + a
            spread(dense_far.at[(h - 1) * group + a], codes_all[q], support_all[q])
            return 0

        return lax.fori_loop(1, groups, from_group, 0)

    if pieces > 1:
        lax.fori_loop(0, group, spread_far, 0)
    for k, m in sharers:
        next_copy(k, m).wait_recv()
    mate_copy().start()
    feed(len(waiting))

    def far_sums(i):
        lanes = slice(i * piece_width, (i + 1) * piece_width)

        def from_region(a, _):
            def from_group(h, _):
                q = other(groups - h) * group + a
                place = 0
                if pieces > 1:
                    place = (groups - h - 1) * group + a
                else:
                    spread(dense_far.at[0], codes_all[q], support_all[q])
                residual_copy(a, h, i).wait_recv()
                far_terms[...] = scale_factor * jnp.dot(
                    dense_far[place], residuals[q, i], preferred_element_type=F32
                )

                def slot(j, _):
                    rows = pl.ds(pl.multiple_of(j * block_width, block_width), block_width)
                    term = far_terms[rows]
                    for r in range(group):
                        sums[r, rows, lanes] += same(base + r, q, j) * term
                    return 0

                return lax.fori_loop(0, owners, slot, 0)

            return lax.fori_loop(1, groups, from_group, 0)

        lax.fori_loop(0, group, from_region, 0)

    def second(i):
        lanes = slice(i * piece_width, (i + 1) * piece_width)

        def region_work(a, _):
            region = base + a
            panel = (
                panels[a, :, :, lanes].reshape(owners * block_width, piece_width).astype(F32)
                + ATOM_RATE * sums[a, :, lanes]
            ).astype(BF16)
            panels_next[a, :, lanes] = panel
            coefficients = dense[a]
            rebuilt = scale_factor * lax.dot_general(
                coefficients, panel, FIRST_TO_FIRST, preferred_element_type=F32
            )
            residual = (pixels[a, :, lanes].astype(F32) - rebuilt).astype(BF16)
            residuals_next[a, :, lanes] = residual
            after = terms[a, :, lanes] + scale_factor * jnp.dot(
                coefficients, residual, preferred_element_type=F32
            )
            term_out[a, i] = after.astype(BF16).reshape(owners, block_width, piece_width)

            @pl.when(a < terms_window)
            def _():
                for j in order:
                    term_copy(a, j, i).start()

            arrived[region, spot, i] = term_out[a, i, me]
            return 0

        lax.fori_loop(0, group, region_work, 0)

    def feed_terms(a, i):
        if terms_window <= a < group:
            for j in order:
                term_copy(a - terms_window, j, i).wait_send()
                term_copy(a, j, i).start()

    def spread_next(a, _):
        spread(dense.at[a], codes_next[a], support_all[base + a])
        return 0

    far_sums(0)
    mate_copy().wait_recv()
    lax.fori_loop(0, group, spread_next, 0)
    second(0)
    for i in range(1, pieces):
        for a in range(group):
            feed_terms(a, i - 1)
        far_sums(i)
        second(i)

    def third(a, _):
        products[...] = lax.dot_general(
            panels_next[a], residuals_next[a], LAST_TO_LAST, preferred_element_type=F32
        )
        pick(1, a, support_all[base + a])
        twin_copy(1, a).start()

        @pl.when(a > 0)
        def _():
            forward(1, a - 1)

        return 0

    lax.fori_loop(0, group, third, 0)
    forward(1, group - 1)
    for a in range(terms_window, group):
        feed_terms(a, pieces - 1)
    reduce_codes(1)
    for j in range(1, pairs):
        row_copy(j).start()
    for j in range(1, pairs):
        row_copy(j).wait_recv()
    last_copy().start()

    def new_blocks(i):
        for a in range(group):
            for j in range(1, owners):
                term_copy(a, j, i).wait_recv()

        def one_slot(r, _):
            for k in range(group):
                start = k * width + i * piece_width
                total = jnp.zeros((block_width, piece_width), F32)
                for q in range(owners):
                    total = total + same(r, q, me) * arrived[q, k, i].astype(F32)
                before = staged[k, r, :, i * piece_width:(i + 1) * piece_width]
                pool[owned + r, :, start:start + piece_width] = (
                    before.astype(F32) + ATOM_RATE * total
                ).astype(BF16)
            return 0

        lax.fori_loop(0, owners, one_slot, 0)

    new_blocks(0)
    last_copy().wait_recv()
    codes_out[...] = master[...].T
    for i in range(1, pieces):
        new_blocks(i)

    def place_block(b, _):
        dictionary_out[b] = pool[chosen[b]]
        return 0

    lax.fori_loop(0, owned, place_block, 0)

    def drain(a, _):
        for step in range(2):
            twin_copy(step, a).wait_send()
        return 0

    lax.fori_loop(0, group, drain, 0)
    for a, i in queue[len(sent):]:
        for h in range(1, groups):
            residual_copy(a, h, i).wait_send()
    for a in range(group):
        for i in range(pieces):
            if a + terms_window >= group:
                for j in order:
                    term_copy(a, j, i).wait_send()
    for j in range(1, owners):
        panel_copy(group - 1, j).wait_send()
        ask_copy(j).wait_send()
        support_copy(j).wait_send()
    for k in range(1, group):
        codes_copy(k).wait_send()
        near_copy(k).wait_send()
        pixel_copy(k).wait_send()
    for k, m in sharers:
        next_copy(k, m).wait_send()
        for step in range(2):
            part_copy(step, k, m).wait_send()
    for j in range(1, pairs):
        row_copy(j).wait_send()
    for h in range(1, groups):
        far_copy(h).wait_send()
        for k in range(1, group):
            fan_copy(h, k).wait_send()
        lift_copy(h).wait_send()
    mate_copy().wait_send()
    last_copy().wait_send()


def group_size(owners, pixel_count):
    group = owners // 2
    while group > 1 and (owners % group or pixel_count % (group * LANES)):
        group //= 2
    return group


def local(patterns, dictionary, codes, support, wanted):
    owners = lax.axis_size("blk")
    row_count = lax.axis_size("rows")
    pattern_rows, pixel_count = patterns.shape
    support_count = support.shape[1]
    code_width = codes.shape[1]
    block_width = code_width // support_count
    owned = dictionary.shape[0] // block_width
    scale_factor = code_width ** (-0.5)
    group = group_size(owners, pixel_count)
    groups = owners // group
    width = pixel_count // group
    pieces = 2 if width % (2 * LANES) == 0 else 1
    piece_width = width // pieces
    share = code_width // 2
    pairs = row_count // 2
    atoms = owners * block_width
    blocks = dictionary.reshape(owned, block_width, pixel_count)
    vmem = pl.BlockSpec(memory_space=pltpu.VMEM)
    hbm = pl.BlockSpec(memory_space=pltpu.HBM)
    dma = pltpu.SemaphoreType.DMA
    dictionary_after, codes_after = pl.pallas_call(
        functools.partial(steps_kernel, owners, row_count, group, pieces, block_width, scale_factor),
        out_shape=(
            jax.ShapeDtypeStruct((owned, block_width, pixel_count), BF16),
            jax.ShapeDtypeStruct((pattern_rows, code_width), F32),
        ),
        in_specs=[hbm] * 5,
        out_specs=(vmem, vmem),
        scratch_shapes=[
            pltpu.VMEM((owned + owners, block_width, pixel_count), BF16),
            pltpu.VMEM(patterns.shape, BF16),
            pltpu.VMEM(codes.shape, BF16),
            pltpu.VMEM((owners,) + support.shape[::-1], jnp.int32),
            pltpu.VMEM((owners,) + wanted.shape, jnp.int32),
            pltpu.SMEM((owners,) + wanted.shape, jnp.int32),
            pltpu.SMEM((owned,), jnp.int32),
            pltpu.VMEM((owners, code_width, pattern_rows), BF16),
            pltpu.VMEM((group, owners, block_width, width), BF16),
            pltpu.VMEM((group, owners, block_width, width), BF16),
            pltpu.VMEM((group, pattern_rows, width), BF16),
            pltpu.VMEM((group, atoms, pattern_rows), BF16),
            pltpu.VMEM((owners - group if pieces > 1 else 1, atoms, pattern_rows), BF16),
            pltpu.VMEM((owners, pieces, pattern_rows, piece_width), BF16),
            pltpu.VMEM((group, atoms, width), F32),
            pltpu.VMEM((group, atoms, width), F32),
            pltpu.VMEM((atoms, pattern_rows), F32),
            pltpu.VMEM((atoms, piece_width), F32),
            pltpu.VMEM((group, atoms, width), BF16),
            pltpu.VMEM((group, pattern_rows, width), BF16),
            pltpu.VMEM((group, pieces, owners, block_width, piece_width), BF16),
            pltpu.VMEM((owners, group, pieces, block_width, piece_width), BF16),
            pltpu.VMEM((2, group, code_width, pattern_rows), BF16),
            pltpu.VMEM((2, group, share, pattern_rows), BF16),
            pltpu.VMEM((2, group, share, pattern_rows), BF16),
            pltpu.VMEM((2, group, pairs, share // pairs, pattern_rows), BF16),
            pltpu.VMEM((code_width, pattern_rows), F32),
            pltpu.VMEM((group, code_width, pattern_rows), BF16),
            dma((6,)),
            dma((owners,)), dma((owners,)),
            dma((owners,)), dma((owners,)),
            dma((group,)), dma((group,)),
            dma((group,)), dma((group,)),
            dma((groups,)), dma((groups,)),
            dma((groups, group)), dma((groups, group)),
            dma((groups,)), dma((groups,)),
            dma((group,)), dma((group,)),
            dma((group, owners)), dma((group, owners)),
            dma((group, groups, pieces)), dma((group, groups, pieces)),
            dma((2, group)), dma((2, group)),
            dma((2, group, pairs)), dma((2, group, pairs)),
            dma((pairs,)), dma((pairs,)),
            dma((group, pairs)), dma((group, pairs)),
            dma((2,)), dma((2,)),
            dma((group, owners, pieces)), dma((group, owners, pieces)),
        ],
        compiler_params=pltpu.CompilerParams(
            collective_id=0, has_side_effects=True, vmem_limit_bytes=49 * 1024 * 1024
        ),
    )(wanted, support.T, codes, patterns, blocks)
    return (dictionary_after.reshape(dictionary.shape), codes_after)


def solution(mesh):
    placed = (P("blk", "rows"), P("blk", "rows"), P("blk", None), P("blk", None), P("blk", None))
    return jax.shard_map(
        local,
        mesh=mesh,
        in_specs=placed,
        out_specs=(P("blk", "rows"), P("blk", None)),
        check_vma=False,
    )
```

```python
import functools

import jax
import jax.numpy as jnp
from jax import lax
from jax.experimental import pallas as pl
from jax.experimental.pallas import tpu as pltpu
from jax.sharding import PartitionSpec as P

CODE_RATE = 0.05
ATOM_RATE = 0.2
LANES = 128
WINDOW = 3
TERMS_WINDOW = 2
PANELS_WINDOW = 3
MESH = pl.DeviceIdType.MESH
F32 = jnp.float32
BF16 = jnp.bfloat16
FIRST_TO_FIRST = (((0,), (0,)), ((), ()))
LAST_TO_LAST = (((1,), (1,)), ((), ()))


def steps_kernel(
    owners, row_count, group, pieces, block_width, scale_factor,
    wanted_hbm, support_hbm, codes_hbm, patterns_hbm, dictionary_hbm,
    dictionary_out, codes_out,
    pool, patterns_ref, codes_ref, support_all, asked_vmem, asked_smem, chosen,
    codes_all, staged, panels, pixels, dense, dense_far, residuals, terms, sums, products,
    far_terms, panels_next, residuals_next, term_out, arrived,
    part_out, twin_in, half_sums, part_in, master, codes_next,
    load_sems, ask_send, ask_recv, support_send, support_recv,
    codes_send, codes_recv, near_send, near_recv, far_send, far_recv, fan_send, fan_recv,
    lift_send, lift_recv, pixel_send, pixel_recv, panel_send, panel_recv,
    residual_send, residual_recv, twin_send, twin_recv, part_send, part_recv,
    row_send, row_recv, next_send, next_recv, mate_send, mate_recv, term_send, term_recv,
):
    me = lax.axis_index("blk")
    my_row = lax.axis_index("rows")
    groups = owners // group
    mine = me // group
    spot = lax.rem(me, group)
    base = mine * group
    owned = dictionary_out.shape[0]
    pattern_rows, pixel_count = patterns_ref.shape
    support_count = support_hbm.shape[0]
    code_width = codes_ref.shape[1]
    width = pixel_count // group
    piece_width = width // pieces
    share = code_width // 2
    core = lax.rem(my_row, 2)
    pair = my_row // 2
    pairs = row_count // 2
    twin = {"rows": pair * 2 + 1 - core}
    kept = pl.ds(pl.multiple_of(core * share, share), share)
    given = pl.ds(pl.multiple_of((1 - core) * share, share), share)
    quarter = share // pairs
    mine_rows = pl.ds(pl.multiple_of(core * share + pair * quarter, quarter), quarter)
    sharers = [(k, m) for m in range(pairs) for k in range(group) if k or m]
    window = min(WINDOW, group)
    panels_window = min(PANELS_WINDOW, group)
    terms_window = min(TERMS_WINDOW, group)
    order = sorted(range(1, owners), key=lambda j: abs(2 * j - owners))

    def columns(k):
        return pl.ds(pl.multiple_of(k * width, width), width)

    loads = (
        pltpu.make_async_copy(wanted_hbm, asked_vmem.at[me], load_sems.at[0]),
        pltpu.make_async_copy(support_hbm, support_all.at[me], load_sems.at[1]),
        pltpu.make_async_copy(codes_hbm, codes_ref, load_sems.at[2]),
        pltpu.make_async_copy(dictionary_hbm, pool.at[pl.ds(0, owned)], load_sems.at[3]),
        pltpu.make_async_copy(patterns_hbm, patterns_ref, load_sems.at[4]),
    )
    for load in loads:
        load.start()

    barrier = pltpu.get_barrier_semaphore()
    for j in range(1, owners):
        pl.semaphore_signal(
            barrier, inc=1, device_id={"blk": lax.rem(me + j, owners)}, device_id_type=MESH
        )
    for j in range(1, row_count):
        pl.semaphore_signal(
            barrier, inc=1, device_id={"rows": lax.rem(my_row + j, row_count)}, device_id_type=MESH
        )
    for k in range(1, group):
        for m in range(1, pairs):
            pl.semaphore_signal(
                barrier, inc=1,
                device_id={"blk": base + lax.rem(spot + k, group),
                           "rows": lax.rem(my_row + 2 * m, row_count)},
                device_id_type=MESH,
            )
    pl.semaphore_wait(barrier, owners + row_count - 2 + (group - 1) * (pairs - 1))

    def remote(source, target, send, recv, device):
        return pltpu.make_async_remote_copy(
            src_ref=source, dst_ref=target, send_sem=send, recv_sem=recv,
            device_id=device, device_id_type=MESH,
        )

    def peer(j):
        return lax.rem(me + j, owners)

    def beside(k):
        return lax.rem(spot + k, group)

    def other(h):
        return lax.rem(mine + h, groups)

    def row_peer(j):
        return {"rows": lax.rem(my_row + 2 * j, row_count)}

    def ask_copy(j):
        return remote(asked_vmem.at[me], asked_vmem.at[me], ask_send.at[j], ask_recv.at[j],
                      {"blk": peer(j)})

    def support_copy(j):
        return remote(support_all.at[me], support_all.at[me], support_send.at[j],
                      support_recv.at[j], {"blk": peer(j)})

    def codes_copy(k):
        part = codes_all.at[me, kept]
        return remote(part, part, codes_send.at[k], codes_recv.at[k],
                      {"blk": base + beside(k)})

    def near_copy(k):
        part = codes_all.at[base + beside(group - k), kept]
        return remote(part, part, near_send.at[k], near_recv.at[k], twin)

    def far_copy(h):
        part = codes_all.at[me, kept]
        return remote(part, part, far_send.at[h], far_recv.at[h],
                      {"blk": other(h) * group + spot})

    def fan_copy(h, k):
        part = codes_all.at[other(groups - h) * group + spot, kept]
        return remote(part, part, fan_send.at[h, k], fan_recv.at[h, k],
                      {"blk": base + beside(k)})

    def lift_copy(h):
        part = codes_all.at[pl.ds(other(h) * group, group), kept]
        return remote(part, part, lift_send.at[h], lift_recv.at[h], twin)

    def pixel_copy(k):
        return remote(patterns_ref.at[:, columns(beside(k))], pixels.at[spot],
                      pixel_send.at[k], pixel_recv.at[k], {"blk": base + beside(k)})

    def panel_copy(a, j):
        to = peer(j)
        return remote(staged.at[lax.rem(to, group), (to // group) * group + a],
                      panels.at[a, me], panel_send.at[a, j], panel_recv.at[a, j], {"blk": to})

    def residual_copy(a, h, i):
        part = residuals.at[base + a, i]
        return remote(part, part, residual_send.at[a, h, i], residual_recv.at[a, h, i],
                      {"blk": other(h) * group + spot})

    def twin_copy(step, a):
        return remote(part_out.at[step, a, given], twin_in.at[step, a],
                      twin_send.at[step, a], twin_recv.at[step, a], twin)

    def sharer(k, m):
        return {"blk": base + beside(k), "rows": lax.rem(my_row + 2 * m, row_count)}

    def part_copy(step, k, m):
        to = lax.rem(pair + m, pairs)
        rows = pl.ds(pl.multiple_of(to * quarter, quarter), quarter)
        return remote(half_sums.at[step, beside(k), rows], part_in.at[step, spot, pair],
                      part_send.at[step, k, m], part_recv.at[step, k, m], sharer(k, m))

    def next_copy(k, m):
        part = codes_next.at[spot, mine_rows]
        return remote(part, part, next_send.at[k, m], next_recv.at[k, m], sharer(k, m))

    def row_copy(j):
        part = master.at[mine_rows]
        return remote(part, part, row_send.at[j], row_recv.at[j], row_peer(j))

    def mate_copy():
        part = codes_next.at[:, kept]
        return remote(part, part, mate_send.at[0], mate_recv.at[0], twin)

    def last_copy():
        part = master.at[kept]
        return remote(part, part, mate_send.at[1], mate_recv.at[1], twin)

    def term_copy(a, j, i):
        to = peer(j)
        return remote(term_out.at[a, i, to], arrived.at[base + a, spot, i],
                      term_send.at[a, j, i], term_recv.at[a, j, i], {"blk": to})

    loads[0].wait()
    for j in order:
        ask_copy(j).start()
    loads[2].wait()
    codes_now = codes_ref[...].astype(F32).T
    master[...] = codes_now
    codes_all[me] = codes_now.astype(BF16)
    for h in range(1, groups):
        far_copy(h).start()
    for k in range(1, group):
        codes_copy(k).start()
    loads[1].wait()
    for j in order:
        support_copy(j).start()
    loads[4].wait()
    for k in range(1, group):
        pixel_copy(k).start()
    pixels[spot] = patterns_ref[:, columns(spot)]

    for j in order:
        ask_copy(j).wait_recv()
    move = pltpu.make_async_copy(asked_vmem, asked_smem, load_sems.at[5])
    move.start()
    move.wait()

    def asked(r, j):
        return asked_smem[r, 0, j]

    def same(r, q, j):
        return jnp.where(asked(r, j) == asked(q, j), 1.0, 0.0).astype(F32)

    loads[3].wait()

    def gather_panels(a):
        def gather(h, _):
            region = h * group + a
            for k in range(group):
                staged[k, region] = pool[asked(region, me), :, k * width:(k + 1) * width]
            return 0

        lax.fori_loop(0, groups, gather, 0)
        panels[a, me] = staged[spot, base + a]

    for a in range(panels_window):
        gather_panels(a)
        for j in order:
            panel_copy(a, j).start()

    def gather_more(a, _):
        gather_panels(a)
        return 0

    lax.fori_loop(panels_window, group, gather_more, 0)

    def choose(b, _):
        place = b
        for r in range(owners):
            place = jnp.where(asked(r, me) == b, owned + r, place)
        chosen[b] = place
        return 0

    lax.fori_loop(0, owned, choose, 0)
    for k in range(1, group):
        codes_copy(k).wait_recv()
        near_copy(k).start()
    for j in range(1, owners):
        support_copy(j).wait_recv()

    def spread(target, codes_t, support_t):
        given_codes = [
            codes_t[s * block_width:(s + 1) * block_width, :].astype(F32)
            for s in range(support_count)
        ]
        for m in range(owners):
            total = jnp.zeros((block_width, pattern_rows), F32)
            for s in range(support_count):
                total = jnp.where(support_t[s:s + 1, :] == m, given_codes[s], total)
            target[m * block_width:(m + 1) * block_width, :] = total.astype(BF16)

    def pick(step, a, support_t):
        for s in range(support_count):
            total = jnp.zeros((block_width, pattern_rows), F32)
            for m in range(owners):
                total = jnp.where(
                    support_t[s:s + 1, :] == m,
                    products[m * block_width:(m + 1) * block_width, :], total,
                )
            part_out[step, a, s * block_width:(s + 1) * block_width, :] = (
                scale_factor * total
            ).astype(BF16)

    def forward(step, a):
        twin_copy(step, a).wait_recv()
        half_sums[step, a] = (
            part_out[step, a, kept].astype(F32) + twin_in[step, a].astype(F32)
        ).astype(BF16)

        k = lax.rem(a - spot + group, group)
        for m in range(1, pairs):
            part_copy(step, k, m).start()

        @pl.when(k > 0)
        def _():
            part_copy(step, k, 0).start()

        @pl.when(k == 0)
        def _():
            rows = pl.ds(pl.multiple_of(pair * quarter, quarter), quarter)
            part_in[step, spot, pair] = half_sums[step, spot, rows]

    def first(a, _):
        region = base + a
        k = lax.rem(spot - a + group, group)

        @pl.when(a + panels_window < group)
        def _():
            for j in order:
                panel_copy(a, j).wait_send()
                panel_copy(a + panels_window, j).start()

        @pl.when(k > 0)
        def _():
            near_copy(k).wait_recv()

        support_t = support_all[region]
        spread(dense.at[a], codes_all[region], support_t)

        @pl.when(k > 0)
        def _():
            pixel_copy(k).wait_recv()

        for j in range(1, owners):
            panel_copy(a, j).wait_recv()
        panel = panels[a].reshape(owners * block_width, width)
        coefficients = dense[a]
        rebuilt = scale_factor * lax.dot_general(
            coefficients, panel, FIRST_TO_FIRST, preferred_element_type=F32
        )
        residual = (pixels[a].astype(F32) - rebuilt).astype(BF16)
        for i in range(pieces):
            residuals[region, i] = residual[:, i * piece_width:(i + 1) * piece_width]

        @pl.when(a < window)
        def _():
            for h in range(1, groups):
                residual_copy(a, h, 0).start()

        products[...] = lax.dot_general(panel, residual, LAST_TO_LAST, preferred_element_type=F32)
        pick(0, a, support_t)
        twin_copy(0, a).start()
        terms[a] = scale_factor * jnp.dot(coefficients, residual, preferred_element_type=F32)

        @pl.when(a > 0)
        def _():
            forward(0, a - 1)

        return 0

    lax.fori_loop(0, group, first, 0)
    queue = [(a, i) for i in range(pieces) for a in range(group)]
    waiting = queue[window:]
    sent = []

    def feed(count):
        for _ in range(count):
            if waiting:
                behind = queue[len(sent)]
                sent.append(behind)
                ahead = waiting.pop(0)
                for h in range(1, groups):
                    residual_copy(behind[0], h, behind[1]).wait_send()
                    residual_copy(ahead[0], h, ahead[1]).start()

    forward(0, group - 1)
    for h in range(1, groups):
        far_copy(h).wait_recv()
        for k in range(1, group):
            fan_copy(h, k).start()
    feed(1)

    def own_sums(a, _):
        def slot(j, _):
            rows = pl.ds(pl.multiple_of(j * block_width, block_width), block_width)
            total = jnp.zeros((block_width, width), F32)
            for q in range(group):
                total = total + same(base + a, base + q, j) * terms[q, rows]
            sums[a, rows] = total
            return 0

        return lax.fori_loop(0, owners, slot, 0)

    lax.fori_loop(0, group, own_sums, 0)
    feed(1)

    def reduce_codes(step):
        for k, m in sharers:
            part_copy(step, k, m).wait_recv()
        total = jnp.zeros((quarter, pattern_rows), F32)
        for k in range(group):
            for m in range(pairs):
                total = total + part_in[step, k, m].astype(F32)
        master[mine_rows] += CODE_RATE * total

    reduce_codes(0)
    codes_next[spot, mine_rows] = master[mine_rows].astype(BF16)
    for k, m in sharers:
        next_copy(k, m).start()
    feed(1)
    for h in range(1, groups):
        for k in range(1, group):
            fan_copy(h, k).wait_recv()
        lift_copy(h).start()
    feed(1)
    for h in range(1, groups):
        lift_copy(h).wait_recv()

    def spread_far(a, _):
        def from_group(h, _):
            q = other(h) * group + a
            spread(dense_far.at[(h - 1) * group + a], codes_all[q], support_all[q])
            return 0

        return lax.fori_loop(1, groups, from_group, 0)

    if pieces > 1:
        lax.fori_loop(0, group, spread_far, 0)
    for k, m in sharers:
        next_copy(k, m).wait_recv()
    mate_copy().start()
    feed(len(waiting))

    def far_sums(i):
        lanes = slice(i * piece_width, (i + 1) * piece_width)

        def from_region(a, _):
            def from_group(h, _):
                q = other(groups - h) * group + a
                place = 0
                if pieces > 1:
                    place = (groups - h - 1) * group + a
                else:
                    spread(dense_far.at[0], codes_all[q], support_all[q])
                residual_copy(a, h, i).wait_recv()
                far_terms[...] = scale_factor * jnp.dot(
                    dense_far[place], residuals[q, i], preferred_element_type=F32
                )

                def slot(j, _):
                    rows = pl.ds(pl.multiple_of(j * block_width, block_width), block_width)
                    term = far_terms[rows]
                    for r in range(group):
                        sums[r, rows, lanes] += same(base + r, q, j) * term
                    return 0

                return lax.fori_loop(0, owners, slot, 0)

            return lax.fori_loop(1, groups, from_group, 0)

        lax.fori_loop(0, group, from_region, 0)

    def second(i):
        lanes = slice(i * piece_width, (i + 1) * piece_width)

        def region_work(a, _):
            region = base + a
            panel = (
                panels[a, :, :, lanes].reshape(owners * block_width, piece_width).astype(F32)
                + ATOM_RATE * sums[a, :, lanes]
            ).astype(BF16)
            panels_next[a, :, lanes] = panel
            coefficients = dense[a]
            rebuilt = scale_factor * lax.dot_general(
                coefficients, panel, FIRST_TO_FIRST, preferred_element_type=F32
            )
            residual = (pixels[a, :, lanes].astype(F32) - rebuilt).astype(BF16)
            residuals_next[a, :, lanes] = residual
            after = terms[a, :, lanes] + scale_factor * jnp.dot(
                coefficients, residual, preferred_element_type=F32
            )
            term_out[a, i] = after.astype(BF16).reshape(owners, block_width, piece_width)

            @pl.when(a < terms_window)
            def _():
                for j in order:
                    term_copy(a, j, i).start()

            arrived[region, spot, i] = term_out[a, i, me]
            return 0

        lax.fori_loop(0, group, region_work, 0)

    def feed_terms(a, i):
        if terms_window <= a < group:
            for j in order:
                term_copy(a - terms_window, j, i).wait_send()
                term_copy(a, j, i).start()

    def spread_next(a, _):
        spread(dense.at[a], codes_next[a], support_all[base + a])
        return 0

    far_sums(0)
    mate_copy().wait_recv()
    lax.fori_loop(0, group, spread_next, 0)
    second(0)
    for i in range(1, pieces):
        for a in range(group):
            feed_terms(a, i - 1)
        far_sums(i)
        second(i)

    def third(a, _):
        products[...] = lax.dot_general(
            panels_next[a], residuals_next[a], LAST_TO_LAST, preferred_element_type=F32
        )
        pick(1, a, support_all[base + a])
        twin_copy(1, a).start()

        @pl.when(a > 0)
        def _():
            forward(1, a - 1)

        return 0

    lax.fori_loop(0, group, third, 0)
    forward(1, group - 1)
    for a in range(terms_window, group):
        feed_terms(a, pieces - 1)
    reduce_codes(1)
    for j in range(1, pairs):
        row_copy(j).start()
    for j in range(1, pairs):
        row_copy(j).wait_recv()
    last_copy().start()

    def gather_terms(i, a_first, a_end, last):
        for a in range(a_first, a_end):
            for j in range(1, owners):
                term_copy(a, j, i).wait_recv()

        def one_slot(r, _):
            rows = pl.ds(pl.multiple_of(r * block_width, block_width), block_width)
            for k in range(group):
                start = k * width + i * piece_width
                if a_first:
                    total = terms[k, rows, :piece_width]
                else:
                    total = jnp.zeros((block_width, piece_width), F32)
                for h in range(groups):
                    for a in range(a_first, a_end):
                        q = h * group + a
                        total = total + same(r, q, me) * arrived[q, k, i].astype(F32)
                if last:
                    before = staged[k, r, :, i * piece_width:(i + 1) * piece_width]
                    pool[owned + r, :, start:start + piece_width] = (
                        before.astype(F32) + ATOM_RATE * total
                    ).astype(BF16)
                else:
                    terms[k, rows, :piece_width] = total
            return 0

        lax.fori_loop(0, owners, one_slot, 0)

    def place(i):
        def place_block(b, _):
            for k in range(group):
                start = k * width + i * piece_width
                dictionary_out[b, :, start:start + piece_width] = (
                    pool[chosen[b], :, start:start + piece_width]
                )
            return 0

        lax.fori_loop(0, owned, place_block, 0)

    for i in range(pieces):
        if i == pieces - 1:
            last_copy().wait_recv()
            codes_out[...] = master[...].T
            gather_terms(i, 0, group - 1, False)
            gather_terms(i, group - 1, group, True)
        else:
            gather_terms(i, 0, group, True)
        place(i)

    def drain(a, _):
        for step in range(2):
            twin_copy(step, a).wait_send()
        return 0

    lax.fori_loop(0, group, drain, 0)
    for a, i in queue[len(sent):]:
        for h in range(1, groups):
            residual_copy(a, h, i).wait_send()
    for a in range(group):
        for i in range(pieces):
            if a + terms_window >= group:
                for j in order:
                    term_copy(a, j, i).wait_send()
    for j in range(1, owners):
        for a in range(group - panels_window, group):
            panel_copy(a, j).wait_send()
        ask_copy(j).wait_send()
        support_copy(j).wait_send()
    for k in range(1, group):
        codes_copy(k).wait_send()
        near_copy(k).wait_send()
        pixel_copy(k).wait_send()
    for k, m in sharers:
        next_copy(k, m).wait_send()
        for step in range(2):
            part_copy(step, k, m).wait_send()
    for j in range(1, pairs):
        row_copy(j).wait_send()
    for h in range(1, groups):
        far_copy(h).wait_send()
        for k in range(1, group):
            fan_copy(h, k).wait_send()
        lift_copy(h).wait_send()
    mate_copy().wait_send()
    last_copy().wait_send()


def group_size(owners, pixel_count):
    group = owners // 2
    while group > 1 and (owners % group or pixel_count % (group * LANES)):
        group //= 2
    return group


def local(patterns, dictionary, codes, support, wanted):
    owners = lax.axis_size("blk")
    row_count = lax.axis_size("rows")
    pattern_rows, pixel_count = patterns.shape
    support_count = support.shape[1]
    code_width = codes.shape[1]
    block_width = code_width // support_count
    owned = dictionary.shape[0] // block_width
    scale_factor = code_width ** (-0.5)
    group = group_size(owners, pixel_count)
    groups = owners // group
    width = pixel_count // group
    pieces = 2 if width % (2 * LANES) == 0 else 1
    piece_width = width // pieces
    share = code_width // 2
    pairs = row_count // 2
    atoms = owners * block_width
    blocks = dictionary.reshape(owned, block_width, pixel_count)
    vmem = pl.BlockSpec(memory_space=pltpu.VMEM)
    hbm = pl.BlockSpec(memory_space=pltpu.HBM)
    dma = pltpu.SemaphoreType.DMA
    dictionary_after, codes_after = pl.pallas_call(
        functools.partial(steps_kernel, owners, row_count, group, pieces, block_width, scale_factor),
        out_shape=(
            jax.ShapeDtypeStruct((owned, block_width, pixel_count), BF16),
            jax.ShapeDtypeStruct((pattern_rows, code_width), F32),
        ),
        in_specs=[hbm] * 5,
        out_specs=(vmem, vmem),
        scratch_shapes=[
            pltpu.VMEM((owned + owners, block_width, pixel_count), BF16),
            pltpu.VMEM(patterns.shape, BF16),
            pltpu.VMEM(codes.shape, BF16),
            pltpu.VMEM((owners,) + support.shape[::-1], jnp.int32),
            pltpu.VMEM((owners,) + wanted.shape, jnp.int32),
            pltpu.SMEM((owners,) + wanted.shape, jnp.int32),
            pltpu.SMEM((owned,), jnp.int32),
            pltpu.VMEM((owners, code_width, pattern_rows), BF16),
            pltpu.VMEM((group, owners, block_width, width), BF16),
            pltpu.VMEM((group, owners, block_width, width), BF16),
            pltpu.VMEM((group, pattern_rows, width), BF16),
            pltpu.VMEM((group, atoms, pattern_rows), BF16),
            pltpu.VMEM((owners - group if pieces > 1 else 1, atoms, pattern_rows), BF16),
            pltpu.VMEM((owners, pieces, pattern_rows, piece_width), BF16),
            pltpu.VMEM((group, atoms, width), F32),
            pltpu.VMEM((group, atoms, width), F32),
            pltpu.VMEM((atoms, pattern_rows), F32),
            pltpu.VMEM((atoms, piece_width), F32),
            pltpu.VMEM((group, atoms, width), BF16),
            pltpu.VMEM((group, pattern_rows, width), BF16),
            pltpu.VMEM((group, pieces, owners, block_width, piece_width), BF16),
            pltpu.VMEM((owners, group, pieces, block_width, piece_width), BF16),
            pltpu.VMEM((2, group, code_width, pattern_rows), BF16),
            pltpu.VMEM((2, group, share, pattern_rows), BF16),
            pltpu.VMEM((2, group, share, pattern_rows), BF16),
            pltpu.VMEM((2, group, pairs, share // pairs, pattern_rows), BF16),
            pltpu.VMEM((code_width, pattern_rows), F32),
            pltpu.VMEM((group, code_width, pattern_rows), BF16),
            dma((6,)),
            dma((owners,)), dma((owners,)),
            dma((owners,)), dma((owners,)),
            dma((group,)), dma((group,)),
            dma((group,)), dma((group,)),
            dma((groups,)), dma((groups,)),
            dma((groups, group)), dma((groups, group)),
            dma((groups,)), dma((groups,)),
            dma((group,)), dma((group,)),
            dma((group, owners)), dma((group, owners)),
            dma((group, groups, pieces)), dma((group, groups, pieces)),
            dma((2, group)), dma((2, group)),
            dma((2, group, pairs)), dma((2, group, pairs)),
            dma((pairs,)), dma((pairs,)),
            dma((group, pairs)), dma((group, pairs)),
            dma((2,)), dma((2,)),
            dma((group, owners, pieces)), dma((group, owners, pieces)),
        ],
        compiler_params=pltpu.CompilerParams(
            collective_id=0, has_side_effects=True, vmem_limit_bytes=49 * 1024 * 1024
        ),
    )(*[pltpu.with_memory_space_constraint(x, pltpu.HBM) for x in (wanted, support.T, codes, patterns, blocks)])
    return (dictionary_after.reshape(dictionary.shape), codes_after)


def solution(mesh):
    placed = (P("blk", "rows"), P("blk", "rows"), P("blk", None), P("blk", None), P("blk", None))
    return jax.shard_map(
        local,
        mesh=mesh,
        in_specs=placed,
        out_specs=(P("blk", "rows"), P("blk", None)),
        check_vma=False,
    )
```

```python
import functools

import jax
import jax.numpy as jnp
from jax import lax
from jax.experimental import pallas as pl
from jax.experimental.pallas import tpu as pltpu
from jax.sharding import PartitionSpec as P

CODE_RATE = 0.05
ATOM_RATE = 0.2
LANES = 128
WINDOW = 3
TERMS_WINDOW = 2
PANELS_WINDOW = 3
MESH = pl.DeviceIdType.MESH
F32 = jnp.float32
BF16 = jnp.bfloat16
FIRST_TO_FIRST = (((0,), (0,)), ((), ()))
LAST_TO_LAST = (((1,), (1,)), ((), ()))


def steps_kernel(
    owners, row_count, group, pieces, block_width, scale_factor,
    wanted_hbm, support_hbm, codes_hbm, patterns_hbm, dictionary_hbm,
    dictionary_out, codes_out,
    pool, patterns_ref, codes_ref, support_all, asked_vmem, asked_smem, chosen,
    codes_all, staged, panels, pixels, dense, dense_far, residuals, terms, sums, products,
    far_terms, panels_next, residuals_next, term_out, arrived,
    part_out, twin_in, half_sums, part_in, master, codes_next,
    load_sems, ask_send, ask_recv, support_send, support_recv,
    codes_send, codes_recv, near_send, near_recv, far_send, far_recv, fan_send, fan_recv,
    lift_send, lift_recv, pixel_send, pixel_recv, panel_send, panel_recv,
    residual_send, residual_recv, twin_send, twin_recv, part_send, part_recv,
    row_send, row_recv, next_send, next_recv, mate_send, mate_recv, term_send, term_recv,
):
    me = lax.axis_index("blk")
    my_row = lax.axis_index("rows")
    groups = owners // group
    mine = me // group
    spot = lax.rem(me, group)
    base = mine * group
    owned = dictionary_out.shape[0]
    pattern_rows, pixel_count = patterns_ref.shape
    support_count = support_hbm.shape[0]
    code_width = codes_ref.shape[1]
    width = pixel_count // group
    piece_width = width // pieces
    share = code_width // 2
    core = lax.rem(my_row, 2)
    pair = my_row // 2
    pairs = row_count // 2
    twin = {"rows": pair * 2 + 1 - core}
    kept = pl.ds(pl.multiple_of(core * share, share), share)
    given = pl.ds(pl.multiple_of((1 - core) * share, share), share)
    quarter = share // pairs
    mine_rows = pl.ds(pl.multiple_of(core * share + pair * quarter, quarter), quarter)
    sharers = [(k, m) for m in range(pairs) for k in range(group) if k or m]
    window = min(WINDOW, group)
    panels_window = min(PANELS_WINDOW, group)
    terms_window = min(TERMS_WINDOW, group)
    order = sorted(range(1, owners), key=lambda j: abs(2 * j - owners))

    def columns(k):
        return pl.ds(pl.multiple_of(k * width, width), width)

    loads = (
        pltpu.make_async_copy(wanted_hbm, asked_vmem.at[me], load_sems.at[0]),
        pltpu.make_async_copy(support_hbm, support_all.at[me], load_sems.at[1]),
        pltpu.make_async_copy(codes_hbm, codes_ref, load_sems.at[2]),
        pltpu.make_async_copy(dictionary_hbm, pool.at[pl.ds(0, owned)], load_sems.at[3]),
        pltpu.make_async_copy(patterns_hbm, patterns_ref, load_sems.at[4]),
    )
    for load in loads:
        load.start()

    barrier = pltpu.get_barrier_semaphore()
    for j in range(1, owners):
        pl.semaphore_signal(
            barrier, inc=1, device_id={"blk": lax.rem(me + j, owners)}, device_id_type=MESH
        )
    for j in range(1, row_count):
        pl.semaphore_signal(
            barrier, inc=1, device_id={"rows": lax.rem(my_row + j, row_count)}, device_id_type=MESH
        )
    for k in range(1, group):
        for m in range(1, pairs):
            pl.semaphore_signal(
                barrier, inc=1,
                device_id={"blk": base + lax.rem(spot + k, group),
                           "rows": lax.rem(my_row + 2 * m, row_count)},
                device_id_type=MESH,
            )
    pl.semaphore_wait(barrier, owners + row_count - 2 + (group - 1) * (pairs - 1))

    def remote(source, target, send, recv, device):
        return pltpu.make_async_remote_copy(
            src_ref=source, dst_ref=target, send_sem=send, recv_sem=recv,
            device_id=device, device_id_type=MESH,
        )

    def peer(j):
        return lax.rem(me + j, owners)

    def beside(k):
        return lax.rem(spot + k, group)

    def other(h):
        return lax.rem(mine + h, groups)

    def row_peer(j):
        return {"rows": lax.rem(my_row + 2 * j, row_count)}

    def ask_copy(j):
        return remote(asked_vmem.at[me], asked_vmem.at[me], ask_send.at[j], ask_recv.at[j],
                      {"blk": peer(j)})

    def support_copy(j):
        return remote(support_all.at[me], support_all.at[me], support_send.at[j],
                      support_recv.at[j], {"blk": peer(j)})

    def codes_copy(k):
        part = codes_all.at[me, kept]
        return remote(part, part, codes_send.at[k], codes_recv.at[k],
                      {"blk": base + beside(k)})

    def near_copy(k):
        part = codes_all.at[base + beside(group - k), kept]
        return remote(part, part, near_send.at[k], near_recv.at[k], twin)

    def far_copy(h):
        part = codes_all.at[me, kept]
        return remote(part, part, far_send.at[h], far_recv.at[h],
                      {"blk": other(h) * group + spot})

    def fan_copy(h, k):
        part = codes_all.at[other(groups - h) * group + spot, kept]
        return remote(part, part, fan_send.at[h, k], fan_recv.at[h, k],
                      {"blk": base + beside(k)})

    def lift_copy(h):
        part = codes_all.at[pl.ds(other(h) * group, group), kept]
        return remote(part, part, lift_send.at[h], lift_recv.at[h], twin)

    def pixel_copy(k):
        return remote(patterns_ref.at[:, columns(beside(k))], pixels.at[spot],
                      pixel_send.at[k], pixel_recv.at[k], {"blk": base + beside(k)})

    def panel_copy(a, j):
        to = peer(j)
        return remote(staged.at[lax.rem(to, group), (to // group) * group + a],
                      panels.at[a, me], panel_send.at[a, j], panel_recv.at[a, j], {"blk": to})

    def residual_copy(a, h, i):
        part = residuals.at[base + a, i]
        return remote(part, part, residual_send.at[a, h, i], residual_recv.at[a, h, i],
                      {"blk": other(h) * group + spot})

    def twin_copy(step, a):
        return remote(part_out.at[step, a, given], twin_in.at[step, a],
                      twin_send.at[step, a], twin_recv.at[step, a], twin)

    def sharer(k, m):
        return {"blk": base + beside(k), "rows": lax.rem(my_row + 2 * m, row_count)}

    def part_copy(step, k, m):
        to = lax.rem(pair + m, pairs)
        rows = pl.ds(pl.multiple_of(to * quarter, quarter), quarter)
        return remote(half_sums.at[step, beside(k), rows], part_in.at[step, spot, pair],
                      part_send.at[step, k, m], part_recv.at[step, k, m], sharer(k, m))

    def next_copy(k, m):
        part = codes_next.at[spot, mine_rows]
        return remote(part, part, next_send.at[k, m], next_recv.at[k, m], sharer(k, m))

    def row_copy(j):
        part = master.at[mine_rows]
        return remote(part, part, row_send.at[j], row_recv.at[j], row_peer(j))

    def mate_copy():
        part = codes_next.at[:, kept]
        return remote(part, part, mate_send.at[0], mate_recv.at[0], twin)

    def last_copy():
        part = master.at[kept]
        return remote(part, part, mate_send.at[1], mate_recv.at[1], twin)

    def term_copy(a, j, i):
        to = peer(j)
        return remote(term_out.at[a, i, to], arrived.at[base + a, spot, i],
                      term_send.at[a, j, i], term_recv.at[a, j, i], {"blk": to})

    loads[0].wait()
    for j in order:
        ask_copy(j).start()
    loads[2].wait()
    codes_now = codes_ref[...].astype(F32).T
    master[...] = codes_now
    codes_all[me] = codes_now.astype(BF16)
    for h in range(1, groups):
        far_copy(h).start()
    for k in range(1, group):
        codes_copy(k).start()
    loads[1].wait()
    for j in order:
        support_copy(j).start()
    loads[4].wait()
    for k in range(1, group):
        pixel_copy(k).start()
    pixels[spot] = patterns_ref[:, columns(spot)]

    for j in order:
        ask_copy(j).wait_recv()
    move = pltpu.make_async_copy(asked_vmem, asked_smem, load_sems.at[5])
    move.start()
    move.wait()

    def asked(r, j):
        return asked_smem[r, 0, j]

    def same(r, q, j):
        return jnp.where(asked(r, j) == asked(q, j), 1.0, 0.0).astype(F32)

    loads[3].wait()

    def gather_panels(a):
        def gather(h, _):
            region = h * group + a
            for k in range(group):
                staged[k, region] = pool[asked(region, me), :, k * width:(k + 1) * width]
            return 0

        lax.fori_loop(0, groups, gather, 0)
        panels[a, me] = staged[spot, base + a]

    for a in range(panels_window):
        gather_panels(a)
        for j in order:
            panel_copy(a, j).start()

    def gather_more(a, _):
        gather_panels(a)
        return 0

    lax.fori_loop(panels_window, group, gather_more, 0)

    def choose(b, _):
        place = b
        for r in range(owners):
            place = jnp.where(asked(r, me) == b, owned + r, place)
        chosen[b] = place
        return 0

    lax.fori_loop(0, owned, choose, 0)
    for k in range(1, group):
        codes_copy(k).wait_recv()
        near_copy(k).start()
    for j in range(1, owners):
        support_copy(j).wait_recv()

    def spread(target, codes_t, support_t):
        given_codes = [
            codes_t[s * block_width:(s + 1) * block_width, :].astype(F32)
            for s in range(support_count)
        ]
        for m in range(owners):
            total = jnp.zeros((block_width, pattern_rows), F32)
            for s in range(support_count):
                total = jnp.where(support_t[s:s + 1, :] == m, given_codes[s], total)
            target[m * block_width:(m + 1) * block_width, :] = total.astype(BF16)

    def pick(step, a, support_t):
        for s in range(support_count):
            total = jnp.zeros((block_width, pattern_rows), F32)
            for m in range(owners):
                total = jnp.where(
                    support_t[s:s + 1, :] == m,
                    products[m * block_width:(m + 1) * block_width, :], total,
                )
            part_out[step, a, s * block_width:(s + 1) * block_width, :] = (
                scale_factor * total
            ).astype(BF16)

    def forward(step, a):
        twin_copy(step, a).wait_recv()
        half_sums[step, a] = (
            part_out[step, a, kept].astype(F32) + twin_in[step, a].astype(F32)
        ).astype(BF16)

        k = lax.rem(a - spot + group, group)
        for m in range(1, pairs):
            part_copy(step, k, m).start()

        @pl.when(k > 0)
        def _():
            part_copy(step, k, 0).start()

        @pl.when(k == 0)
        def _():
            rows = pl.ds(pl.multiple_of(pair * quarter, quarter), quarter)
            part_in[step, spot, pair] = half_sums[step, spot, rows]

    def first(a, _):
        region = base + a
        k = lax.rem(spot - a + group, group)

        @pl.when(a + panels_window < group)
        def _():
            for j in order:
                panel_copy(a, j).wait_send()
                panel_copy(a + panels_window, j).start()

        @pl.when(k > 0)
        def _():
            near_copy(k).wait_recv()

        support_t = support_all[region]
        spread(dense.at[a], codes_all[region], support_t)

        @pl.when(k > 0)
        def _():
            pixel_copy(k).wait_recv()

        for j in range(1, owners):
            panel_copy(a, j).wait_recv()
        panel = panels[a].reshape(owners * block_width, width)
        coefficients = dense[a]
        rebuilt = scale_factor * lax.dot_general(
            coefficients, panel, FIRST_TO_FIRST, preferred_element_type=F32
        )
        residual = (pixels[a].astype(F32) - rebuilt).astype(BF16)
        for i in range(pieces):
            residuals[region, i] = residual[:, i * piece_width:(i + 1) * piece_width]

        @pl.when(a < window)
        def _():
            for h in range(1, groups):
                residual_copy(a, h, 0).start()

        products[...] = lax.dot_general(panel, residual, LAST_TO_LAST, preferred_element_type=F32)
        pick(0, a, support_t)
        twin_copy(0, a).start()
        terms[a] = scale_factor * jnp.dot(coefficients, residual, preferred_element_type=F32)

        @pl.when(a > 0)
        def _():
            forward(0, a - 1)

        return 0

    lax.fori_loop(0, group, first, 0)
    queue = [(a, i) for i in range(pieces) for a in range(group)]
    waiting = queue[window:]
    sent = []

    def feed(count):
        for _ in range(count):
            if waiting:
                behind = queue[len(sent)]
                sent.append(behind)
                ahead = waiting.pop(0)
                for h in range(1, groups):
                    residual_copy(behind[0], h, behind[1]).wait_send()
                    residual_copy(ahead[0], h, ahead[1]).start()

    forward(0, group - 1)
    for h in range(1, groups):
        far_copy(h).wait_recv()
        for k in range(1, group):
            fan_copy(h, k).start()
    feed(1)

    def own_sums(a, _):
        def slot(j, _):
            rows = pl.ds(pl.multiple_of(j * block_width, block_width), block_width)
            total = jnp.zeros((block_width, width), F32)
            for q in range(group):
                total = total + same(base + a, base + q, j) * terms[q, rows]
            sums[a, rows] = total
            return 0

        return lax.fori_loop(0, owners, slot, 0)

    lax.fori_loop(0, group, own_sums, 0)
    feed(1)

    def reduce_codes(step):
        for k, m in sharers:
            part_copy(step, k, m).wait_recv()
        total = jnp.zeros((quarter, pattern_rows), F32)
        for k in range(group):
            for m in range(pairs):
                total = total + part_in[step, k, m].astype(F32)
        master[mine_rows] += CODE_RATE * total

    reduce_codes(0)
    codes_next[spot, mine_rows] = master[mine_rows].astype(BF16)
    for k, m in sharers:
        next_copy(k, m).start()
    feed(1)
    for h in range(1, groups):
        for k in range(1, group):
            fan_copy(h, k).wait_recv()
        lift_copy(h).start()
    feed(1)
    for h in range(1, groups):
        lift_copy(h).wait_recv()

    def spread_far(a, _):
        def from_group(h, _):
            q = other(h) * group + a
            spread(dense_far.at[(h - 1) * group + a], codes_all[q], support_all[q])
            return 0

        return lax.fori_loop(1, groups, from_group, 0)

    if pieces > 1:
        lax.fori_loop(0, group, spread_far, 0)
    feed(len(waiting))

    def far_sums(i):
        lanes = slice(i * piece_width, (i + 1) * piece_width)

        def from_region(a, _):
            def from_group(h, _):
                q = other(groups - h) * group + a
                place = 0
                if pieces > 1:
                    place = (groups - h - 1) * group + a
                else:
                    spread(dense_far.at[0], codes_all[q], support_all[q])
                residual_copy(a, h, i).wait_recv()
                far_terms[...] = scale_factor * jnp.dot(
                    dense_far[place], residuals[q, i], preferred_element_type=F32
                )

                def slot(j, _):
                    rows = pl.ds(pl.multiple_of(j * block_width, block_width), block_width)
                    term = far_terms[rows]
                    for r in range(group):
                        sums[r, rows, lanes] += same(base + r, q, j) * term
                    return 0

                return lax.fori_loop(0, owners, slot, 0)

            return lax.fori_loop(1, groups, from_group, 0)

        lax.fori_loop(0, group, from_region, 0)

    def second(i):
        lanes = slice(i * piece_width, (i + 1) * piece_width)

        def region_work(a, _):
            region = base + a
            if i == 0:
                spread(dense.at[a], codes_next[a], support_all[region])
            panel = (
                panels[a, :, :, lanes].reshape(owners * block_width, piece_width).astype(F32)
                + ATOM_RATE * sums[a, :, lanes]
            ).astype(BF16)
            panels_next[a, :, lanes] = panel
            coefficients = dense[a]
            rebuilt = scale_factor * lax.dot_general(
                coefficients, panel, FIRST_TO_FIRST, preferred_element_type=F32
            )
            residual = (pixels[a, :, lanes].astype(F32) - rebuilt).astype(BF16)
            residuals_next[a, :, lanes] = residual
            after = terms[a, :, lanes] + scale_factor * jnp.dot(
                coefficients, residual, preferred_element_type=F32
            )
            term_out[a, i] = after.astype(BF16).reshape(owners, block_width, piece_width)

            @pl.when(a < terms_window)
            def _():
                for j in order:
                    term_copy(a, j, i).start()

            arrived[region, spot, i] = term_out[a, i, me]
            return 0

        lax.fori_loop(0, group, region_work, 0)

    def feed_terms(a, i):
        if terms_window <= a < group:
            for j in order:
                term_copy(a - terms_window, j, i).wait_send()
                term_copy(a, j, i).start()

    far_sums(0)
    for k, m in sharers:
        next_copy(k, m).wait_recv()
    mate_copy().start()
    mate_copy().wait_recv()
    second(0)
    for i in range(1, pieces):
        for a in range(group):
            feed_terms(a, i - 1)
        far_sums(i)
        second(i)

    def third(a, _):
        products[...] = lax.dot_general(
            panels_next[a], residuals_next[a], LAST_TO_LAST, preferred_element_type=F32
        )
        pick(1, a, support_all[base + a])
        twin_copy(1, a).start()

        @pl.when(a > 0)
        def _():
            forward(1, a - 1)

        return 0

    lax.fori_loop(0, group, third, 0)
    forward(1, group - 1)
    for a in range(terms_window, group):
        feed_terms(a, pieces - 1)
    reduce_codes(1)
    for j in range(1, pairs):
        row_copy(j).start()
    for j in range(1, pairs):
        row_copy(j).wait_recv()
    last_copy().start()

    def gather_terms(i, a_first, a_end, last):
        for a in range(a_first, a_end):
            for j in range(1, owners):
                term_copy(a, j, i).wait_recv()

        def one_slot(r, _):
            rows = pl.ds(pl.multiple_of(r * block_width, block_width), block_width)
            for k in range(group):
                start = k * width + i * piece_width
                if a_first:
                    total = terms[k, rows, :piece_width]
                else:
                    total = jnp.zeros((block_width, piece_width), F32)
                for h in range(groups):
                    for a in range(a_first, a_end):
                        q = h * group + a
                        total = total + same(r, q, me) * arrived[q, k, i].astype(F32)
                if last:
                    before = staged[k, r, :, i * piece_width:(i + 1) * piece_width]
                    pool[owned + r, :, start:start + piece_width] = (
                        before.astype(F32) + ATOM_RATE * total
                    ).astype(BF16)
                else:
                    terms[k, rows, :piece_width] = total
            return 0

        lax.fori_loop(0, owners, one_slot, 0)

    def place(i):
        def place_block(b, _):
            for k in range(group):
                start = k * width + i * piece_width
                dictionary_out[b, :, start:start + piece_width] = (
                    pool[chosen[b], :, start:start + piece_width]
                )
            return 0

        lax.fori_loop(0, owned, place_block, 0)

    for i in range(pieces):
        if i == pieces - 1:
            last_copy().wait_recv()
            codes_out[...] = master[...].T
            gather_terms(i, 0, group - 1, False)
            gather_terms(i, group - 1, group, True)
        else:
            gather_terms(i, 0, group, True)
        place(i)

    def drain(a, _):
        for step in range(2):
            twin_copy(step, a).wait_send()
        return 0

    lax.fori_loop(0, group, drain, 0)
    for a, i in queue[len(sent):]:
        for h in range(1, groups):
            residual_copy(a, h, i).wait_send()
    for a in range(group):
        for i in range(pieces):
            if a + terms_window >= group:
                for j in order:
                    term_copy(a, j, i).wait_send()
    for j in range(1, owners):
        for a in range(group - panels_window, group):
            panel_copy(a, j).wait_send()
        ask_copy(j).wait_send()
        support_copy(j).wait_send()
    for k in range(1, group):
        codes_copy(k).wait_send()
        near_copy(k).wait_send()
        pixel_copy(k).wait_send()
    for k, m in sharers:
        next_copy(k, m).wait_send()
        for step in range(2):
            part_copy(step, k, m).wait_send()
    for j in range(1, pairs):
        row_copy(j).wait_send()
    for h in range(1, groups):
        far_copy(h).wait_send()
        for k in range(1, group):
            fan_copy(h, k).wait_send()
        lift_copy(h).wait_send()
    mate_copy().wait_send()
    last_copy().wait_send()


def group_size(owners, pixel_count):
    group = owners // 2
    while group > 1 and (owners % group or pixel_count % (group * LANES)):
        group //= 2
    return group


def local(patterns, dictionary, codes, support, wanted):
    owners = lax.axis_size("blk")
    row_count = lax.axis_size("rows")
    pattern_rows, pixel_count = patterns.shape
    support_count = support.shape[1]
    code_width = codes.shape[1]
    block_width = code_width // support_count
    owned = dictionary.shape[0] // block_width
    scale_factor = code_width ** (-0.5)
    group = group_size(owners, pixel_count)
    groups = owners // group
    width = pixel_count // group
    pieces = 2 if width % (2 * LANES) == 0 else 1
    piece_width = width // pieces
    share = code_width // 2
    pairs = row_count // 2
    atoms = owners * block_width
    blocks = dictionary.reshape(owned, block_width, pixel_count)
    vmem = pl.BlockSpec(memory_space=pltpu.VMEM)
    hbm = pl.BlockSpec(memory_space=pltpu.HBM)
    dma = pltpu.SemaphoreType.DMA
    dictionary_after, codes_after = pl.pallas_call(
        functools.partial(steps_kernel, owners, row_count, group, pieces, block_width, scale_factor),
        out_shape=(
            jax.ShapeDtypeStruct((owned, block_width, pixel_count), BF16),
            jax.ShapeDtypeStruct((pattern_rows, code_width), F32),
        ),
        in_specs=[hbm] * 5,
        out_specs=(vmem, vmem),
        scratch_shapes=[
            pltpu.VMEM((owned + owners, block_width, pixel_count), BF16),
            pltpu.VMEM(patterns.shape, BF16),
            pltpu.VMEM(codes.shape, BF16),
            pltpu.VMEM((owners,) + support.shape[::-1], jnp.int32),
            pltpu.VMEM((owners,) + wanted.shape, jnp.int32),
            pltpu.SMEM((owners,) + wanted.shape, jnp.int32),
            pltpu.SMEM((owned,), jnp.int32),
            pltpu.VMEM((owners, code_width, pattern_rows), BF16),
            pltpu.VMEM((group, owners, block_width, width), BF16),
            pltpu.VMEM((group, owners, block_width, width), BF16),
            pltpu.VMEM((group, pattern_rows, width), BF16),
            pltpu.VMEM((group, atoms, pattern_rows), BF16),
            pltpu.VMEM((owners - group if pieces > 1 else 1, atoms, pattern_rows), BF16),
            pltpu.VMEM((owners, pieces, pattern_rows, piece_width), BF16),
            pltpu.VMEM((group, atoms, width), F32),
            pltpu.VMEM((group, atoms, width), F32),
            pltpu.VMEM((atoms, pattern_rows), F32),
            pltpu.VMEM((atoms, piece_width), F32),
            pltpu.VMEM((group, atoms, width), BF16),
            pltpu.VMEM((group, pattern_rows, width), BF16),
            pltpu.VMEM((group, pieces, owners, block_width, piece_width), BF16),
            pltpu.VMEM((owners, group, pieces, block_width, piece_width), BF16),
            pltpu.VMEM((2, group, code_width, pattern_rows), BF16),
            pltpu.VMEM((2, group, share, pattern_rows), BF16),
            pltpu.VMEM((2, group, share, pattern_rows), BF16),
            pltpu.VMEM((2, group, pairs, share // pairs, pattern_rows), BF16),
            pltpu.VMEM((code_width, pattern_rows), F32),
            pltpu.VMEM((group, code_width, pattern_rows), BF16),
            dma((6,)),
            dma((owners,)), dma((owners,)),
            dma((owners,)), dma((owners,)),
            dma((group,)), dma((group,)),
            dma((group,)), dma((group,)),
            dma((groups,)), dma((groups,)),
            dma((groups, group)), dma((groups, group)),
            dma((groups,)), dma((groups,)),
            dma((group,)), dma((group,)),
            dma((group, owners)), dma((group, owners)),
            dma((group, groups, pieces)), dma((group, groups, pieces)),
            dma((2, group)), dma((2, group)),
            dma((2, group, pairs)), dma((2, group, pairs)),
            dma((pairs,)), dma((pairs,)),
            dma((group, pairs)), dma((group, pairs)),
            dma((2,)), dma((2,)),
            dma((group, owners, pieces)), dma((group, owners, pieces)),
        ],
        compiler_params=pltpu.CompilerParams(
            collective_id=0, has_side_effects=True, vmem_limit_bytes=49 * 1024 * 1024
        ),
    )(*[pltpu.with_memory_space_constraint(x, pltpu.HBM) for x in (wanted, support.T, codes, patterns, blocks)])
    return (dictionary_after.reshape(dictionary.shape), codes_after)


def solution(mesh):
    placed = (P("blk", "rows"), P("blk", "rows"), P("blk", None), P("blk", None), P("blk", None))
    return jax.shard_map(
        local,
        mesh=mesh,
        in_specs=placed,
        out_specs=(P("blk", "rows"), P("blk", None)),
        check_vma=False,
    )
```

```python
import functools

import jax
import jax.numpy as jnp
from jax import lax
from jax.experimental import pallas as pl
from jax.experimental.pallas import tpu as pltpu
from jax.sharding import PartitionSpec as P

CODE_RATE = 0.05
ATOM_RATE = 0.2
LANES = 128
WINDOW = 3
TERMS_WINDOW = 3
PANELS_WINDOW = 3
MESH = pl.DeviceIdType.MESH
F32 = jnp.float32
BF16 = jnp.bfloat16
FIRST_TO_FIRST = (((0,), (0,)), ((), ()))
LAST_TO_LAST = (((1,), (1,)), ((), ()))


def steps_kernel(
    owners, row_count, group, pieces, block_width, scale_factor,
    wanted_hbm, support_hbm, codes_hbm, patterns_hbm, dictionary_hbm,
    dictionary_out, codes_out,
    pool, patterns_ref, codes_ref, support_all, asked_vmem, asked_smem, chosen,
    codes_all, staged, panels, pixels, dense, dense_far, residuals, terms, sums, products,
    far_terms, panels_next, residuals_next, term_out, arrived,
    part_out, twin_in, half_sums, part_in, master, codes_next,
    load_sems, ask_send, ask_recv, support_send, support_recv,
    codes_send, codes_recv, near_send, near_recv, far_send, far_recv, fan_send, fan_recv,
    lift_send, lift_recv, pixel_send, pixel_recv, panel_send, panel_recv,
    residual_send, residual_recv, twin_send, twin_recv, part_send, part_recv,
    row_send, row_recv, next_send, next_recv, mate_send, mate_recv, term_send, term_recv,
):
    me = lax.axis_index("blk")
    my_row = lax.axis_index("rows")
    groups = owners // group
    mine = me // group
    spot = lax.rem(me, group)
    base = mine * group
    owned = dictionary_out.shape[0]
    pattern_rows, pixel_count = patterns_ref.shape
    support_count = support_hbm.shape[0]
    code_width = codes_ref.shape[1]
    width = pixel_count // group
    piece_width = width // pieces
    share = code_width // 2
    core = lax.rem(my_row, 2)
    pair = my_row // 2
    pairs = row_count // 2
    twin = {"rows": pair * 2 + 1 - core}
    kept = pl.ds(pl.multiple_of(core * share, share), share)
    given = pl.ds(pl.multiple_of((1 - core) * share, share), share)
    quarter = share // pairs
    mine_rows = pl.ds(pl.multiple_of(core * share + pair * quarter, quarter), quarter)
    sharers = [(k, m) for m in range(pairs) for k in range(group) if k or m]
    window = min(WINDOW, group)
    panels_window = min(PANELS_WINDOW, group)
    terms_window = min(TERMS_WINDOW, group)
    order = sorted(range(1, owners), key=lambda j: abs(2 * j - owners))

    def columns(k):
        return pl.ds(pl.multiple_of(k * width, width), width)

    loads = (
        pltpu.make_async_copy(wanted_hbm, asked_vmem.at[me], load_sems.at[0]),
        pltpu.make_async_copy(support_hbm, support_all.at[me], load_sems.at[1]),
        pltpu.make_async_copy(codes_hbm, codes_ref, load_sems.at[2]),
        pltpu.make_async_copy(dictionary_hbm, pool.at[pl.ds(0, owned)], load_sems.at[3]),
        pltpu.make_async_copy(patterns_hbm, patterns_ref, load_sems.at[4]),
    )
    for load in loads:
        load.start()

    barrier = pltpu.get_barrier_semaphore()
    for j in range(1, owners):
        pl.semaphore_signal(
            barrier, inc=1, device_id={"blk": lax.rem(me + j, owners)}, device_id_type=MESH
        )
    for j in range(1, row_count):
        pl.semaphore_signal(
            barrier, inc=1, device_id={"rows": lax.rem(my_row + j, row_count)}, device_id_type=MESH
        )
    for k in range(1, group):
        for m in range(1, pairs):
            pl.semaphore_signal(
                barrier, inc=1,
                device_id={"blk": base + lax.rem(spot + k, group),
                           "rows": lax.rem(my_row + 2 * m, row_count)},
                device_id_type=MESH,
            )
    pl.semaphore_wait(barrier, owners + row_count - 2 + (group - 1) * (pairs - 1))

    def remote(source, target, send, recv, device):
        return pltpu.make_async_remote_copy(
            src_ref=source, dst_ref=target, send_sem=send, recv_sem=recv,
            device_id=device, device_id_type=MESH,
        )

    def peer(j):
        return lax.rem(me + j, owners)

    def beside(k):
        return lax.rem(spot + k, group)

    def other(h):
        return lax.rem(mine + h, groups)

    def row_peer(j):
        return {"rows": lax.rem(my_row + 2 * j, row_count)}

    def ask_copy(j):
        return remote(asked_vmem.at[me], asked_vmem.at[me], ask_send.at[j], ask_recv.at[j],
                      {"blk": peer(j)})

    def support_copy(j):
        return remote(support_all.at[me], support_all.at[me], support_send.at[j],
                      support_recv.at[j], {"blk": peer(j)})

    def codes_copy(k):
        part = codes_all.at[me, kept]
        return remote(part, part, codes_send.at[k], codes_recv.at[k],
                      {"blk": base + beside(k)})

    def near_copy(k):
        part = codes_all.at[base + beside(group - k), kept]
        return remote(part, part, near_send.at[k], near_recv.at[k], twin)

    def far_copy(h):
        part = codes_all.at[me, kept]
        return remote(part, part, far_send.at[h], far_recv.at[h],
                      {"blk": other(h) * group + spot})

    def fan_copy(h, k):
        part = codes_all.at[other(groups - h) * group + spot, kept]
        return remote(part, part, fan_send.at[h, k], fan_recv.at[h, k],
                      {"blk": base + beside(k)})

    def lift_copy(h):
        part = codes_all.at[pl.ds(other(h) * group, group), kept]
        return remote(part, part, lift_send.at[h], lift_recv.at[h], twin)

    def pixel_copy(k):
        return remote(patterns_ref.at[:, columns(beside(k))], pixels.at[spot],
                      pixel_send.at[k], pixel_recv.at[k], {"blk": base + beside(k)})

    def panel_copy(a, j):
        to = peer(j)
        return remote(staged.at[lax.rem(to, group), (to // group) * group + a],
                      panels.at[a, me], panel_send.at[a, j], panel_recv.at[a, j], {"blk": to})

    def residual_copy(a, h, i):
        part = residuals.at[base + a, i]
        return remote(part, part, residual_send.at[a, h, i], residual_recv.at[a, h, i],
                      {"blk": other(h) * group + spot})

    def twin_copy(step, a):
        return remote(part_out.at[step, a, given], twin_in.at[step, a],
                      twin_send.at[step, a], twin_recv.at[step, a], twin)

    def sharer(k, m):
        return {"blk": base + beside(k), "rows": lax.rem(my_row + 2 * m, row_count)}

    def part_copy(step, k, m):
        to = lax.rem(pair + m, pairs)
        rows = pl.ds(pl.multiple_of(to * quarter, quarter), quarter)
        return remote(half_sums.at[step, beside(k), rows], part_in.at[step, spot, pair],
                      part_send.at[step, k, m], part_recv.at[step, k, m], sharer(k, m))

    def next_copy(k, m):
        part = codes_next.at[spot, mine_rows]
        return remote(part, part, next_send.at[k, m], next_recv.at[k, m], sharer(k, m))

    def row_copy(j):
        part = master.at[mine_rows]
        return remote(part, part, row_send.at[j], row_recv.at[j], row_peer(j))

    def mate_copy():
        part = codes_next.at[:, kept]
        return remote(part, part, mate_send.at[0], mate_recv.at[0], twin)

    def last_copy():
        part = master.at[kept]
        return remote(part, part, mate_send.at[1], mate_recv.at[1], twin)

    def term_copy(a, j, i):
        to = peer(j)
        return remote(term_out.at[a, i, to], arrived.at[base + a, spot, i],
                      term_send.at[a, j, i], term_recv.at[a, j, i], {"blk": to})

    loads[0].wait()
    for j in order:
        ask_copy(j).start()
    loads[2].wait()
    codes_now = codes_ref[...].astype(F32).T
    master[...] = codes_now
    codes_all[me] = codes_now.astype(BF16)
    for h in range(1, groups):
        far_copy(h).start()
    for k in range(1, group):
        codes_copy(k).start()
    loads[1].wait()
    for j in order:
        support_copy(j).start()
    loads[4].wait()
    for k in range(1, group):
        pixel_copy(k).start()
    pixels[spot] = patterns_ref[:, columns(spot)]

    for j in order:
        ask_copy(j).wait_recv()
    move = pltpu.make_async_copy(asked_vmem, asked_smem, load_sems.at[5])
    move.start()
    move.wait()

    def asked(r, j):
        return asked_smem[r, 0, j]

    def same(r, q, j):
        return jnp.where(asked(r, j) == asked(q, j), 1.0, 0.0).astype(F32)

    loads[3].wait()

    def gather_panels(a):
        def gather(h, _):
            region = h * group + a
            for k in range(group):
                staged[k, region] = pool[asked(region, me), :, k * width:(k + 1) * width]
            return 0

        lax.fori_loop(0, groups, gather, 0)
        panels[a, me] = staged[spot, base + a]

    for a in range(panels_window):
        gather_panels(a)
        for j in order:
            panel_copy(a, j).start()

    def gather_more(a, _):
        gather_panels(a)
        return 0

    lax.fori_loop(panels_window, group, gather_more, 0)

    def choose(b, _):
        place = b
        for r in range(owners):
            place = jnp.where(asked(r, me) == b, owned + r, place)
        chosen[b] = place
        return 0

    lax.fori_loop(0, owned, choose, 0)
    for k in range(1, group):
        codes_copy(k).wait_recv()
        near_copy(k).start()
    for j in range(1, owners):
        support_copy(j).wait_recv()

    def spread(target, codes_t, support_t):
        given_codes = [
            codes_t[s * block_width:(s + 1) * block_width, :].astype(F32)
            for s in range(support_count)
        ]
        for m in range(owners):
            total = jnp.zeros((block_width, pattern_rows), F32)
            for s in range(support_count):
                total = jnp.where(support_t[s:s + 1, :] == m, given_codes[s], total)
            target[m * block_width:(m + 1) * block_width, :] = total.astype(BF16)

    def pick(step, a, support_t):
        for s in range(support_count):
            total = jnp.zeros((block_width, pattern_rows), F32)
            for m in range(owners):
                total = jnp.where(
                    support_t[s:s + 1, :] == m,
                    products[m * block_width:(m + 1) * block_width, :], total,
                )
            part_out[step, a, s * block_width:(s + 1) * block_width, :] = (
                scale_factor * total
            ).astype(BF16)

    def forward(step, a):
        twin_copy(step, a).wait_recv()
        half_sums[step, a] = (
            part_out[step, a, kept].astype(F32) + twin_in[step, a].astype(F32)
        ).astype(BF16)

        k = lax.rem(a - spot + group, group)
        for m in range(1, pairs):
            part_copy(step, k, m).start()

        @pl.when(k > 0)
        def _():
            part_copy(step, k, 0).start()

        @pl.when(k == 0)
        def _():
            rows = pl.ds(pl.multiple_of(pair * quarter, quarter), quarter)
            part_in[step, spot, pair] = half_sums[step, spot, rows]

    def first(a, _):
        region = base + a
        k = lax.rem(spot - a + group, group)

        @pl.when(a + panels_window < group)
        def _():
            for j in order:
                panel_copy(a, j).wait_send()
                panel_copy(a + panels_window, j).start()

        @pl.when(k > 0)
        def _():
            near_copy(k).wait_recv()

        support_t = support_all[region]
        spread(dense.at[a], codes_all[region], support_t)

        @pl.when(k > 0)
        def _():
            pixel_copy(k).wait_recv()

        for j in range(1, owners):
            panel_copy(a, j).wait_recv()
        panel = panels[a].reshape(owners * block_width, width)
        coefficients = dense[a]
        rebuilt = scale_factor * lax.dot_general(
            coefficients, panel, FIRST_TO_FIRST, preferred_element_type=F32
        )
        residual = (pixels[a].astype(F32) - rebuilt).astype(BF16)
        for i in range(pieces):
            residuals[region, i] = residual[:, i * piece_width:(i + 1) * piece_width]

        @pl.when(a < window)
        def _():
            for h in range(1, groups):
                residual_copy(a, h, 0).start()

        products[...] = lax.dot_general(panel, residual, LAST_TO_LAST, preferred_element_type=F32)
        pick(0, a, support_t)
        twin_copy(0, a).start()
        terms[a] = scale_factor * jnp.dot(coefficients, residual, preferred_element_type=F32)

        @pl.when(a > 0)
        def _():
            forward(0, a - 1)

        return 0

    lax.fori_loop(0, group, first, 0)
    queue = [(a, i) for i in range(pieces) for a in range(group)]
    waiting = queue[window:]
    sent = []

    def feed(count):
        for _ in range(count):
            if waiting:
                behind = queue[len(sent)]
                sent.append(behind)
                ahead = waiting.pop(0)
                for h in range(1, groups):
                    residual_copy(behind[0], h, behind[1]).wait_send()
                    residual_copy(ahead[0], h, ahead[1]).start()

    forward(0, group - 1)
    for h in range(1, groups):
        far_copy(h).wait_recv()
        for k in range(1, group):
            fan_copy(h, k).start()
    feed(1)

    def own_sums(a, _):
        def slot(j, _):
            rows = pl.ds(pl.multiple_of(j * block_width, block_width), block_width)
            total = jnp.zeros((block_width, width), F32)
            for q in range(group):
                total = total + same(base + a, base + q, j) * terms[q, rows]
            sums[a, rows] = total
            return 0

        return lax.fori_loop(0, owners, slot, 0)

    lax.fori_loop(0, group, own_sums, 0)
    feed(1)

    def reduce_codes(step):
        for k, m in sharers:
            part_copy(step, k, m).wait_recv()
        total = jnp.zeros((quarter, pattern_rows), F32)
        for k in range(group):
            for m in range(pairs):
                total = total + part_in[step, k, m].astype(F32)
        master[mine_rows] += CODE_RATE * total

    reduce_codes(0)
    codes_next[spot, mine_rows] = master[mine_rows].astype(BF16)
    for k, m in sharers:
        next_copy(k, m).start()
    feed(1)
    for h in range(1, groups):
        for k in range(1, group):
            fan_copy(h, k).wait_recv()
        lift_copy(h).start()
    feed(1)
    for h in range(1, groups):
        lift_copy(h).wait_recv()

    def spread_far(a, _):
        def from_group(h, _):
            q = other(h) * group + a
            spread(dense_far.at[(h - 1) * group + a], codes_all[q], support_all[q])
            return 0

        return lax.fori_loop(1, groups, from_group, 0)

    if pieces > 1:
        lax.fori_loop(0, group, spread_far, 0)
    feed(len(waiting))

    def far_sums(i):
        lanes = slice(i * piece_width, (i + 1) * piece_width)

        def from_region(a, _):
            def from_group(h, _):
                q = other(groups - h) * group + a
                place = 0
                if pieces > 1:
                    place = (groups - h - 1) * group + a
                else:
                    spread(dense_far.at[0], codes_all[q], support_all[q])
                residual_copy(a, h, i).wait_recv()
                far_terms[...] = scale_factor * jnp.dot(
                    dense_far[place], residuals[q, i], preferred_element_type=F32
                )

                def slot(j, _):
                    rows = pl.ds(pl.multiple_of(j * block_width, block_width), block_width)
                    term = far_terms[rows]
                    for r in range(group):
                        sums[r, rows, lanes] += same(base + r, q, j) * term
                    return 0

                return lax.fori_loop(0, owners, slot, 0)

            return lax.fori_loop(1, groups, from_group, 0)

        lax.fori_loop(0, group, from_region, 0)

    def second(i):
        lanes = slice(i * piece_width, (i + 1) * piece_width)

        def region_work(a, _):
            region = base + a
            if i == 0:
                spread(dense.at[a], codes_next[a], support_all[region])
            panel = (
                panels[a, :, :, lanes].reshape(owners * block_width, piece_width).astype(F32)
                + ATOM_RATE * sums[a, :, lanes]
            ).astype(BF16)
            panels_next[a, :, lanes] = panel
            coefficients = dense[a]
            rebuilt = scale_factor * lax.dot_general(
                coefficients, panel, FIRST_TO_FIRST, preferred_element_type=F32
            )
            residual = (pixels[a, :, lanes].astype(F32) - rebuilt).astype(BF16)
            residuals_next[a, :, lanes] = residual
            after = terms[a, :, lanes] + scale_factor * jnp.dot(
                coefficients, residual, preferred_element_type=F32
            )
            term_out[a, i] = after.astype(BF16).reshape(owners, block_width, piece_width)

            @pl.when(a < terms_window)
            def _():
                for j in order:
                    term_copy(a, j, i).start()

            arrived[region, spot, i] = term_out[a, i, me]
            return 0

        lax.fori_loop(0, group, region_work, 0)

    def feed_terms(a, i):
        if terms_window <= a < group:
            for j in order:
                term_copy(a - terms_window, j, i).wait_send()
                term_copy(a, j, i).start()

    far_sums(0)
    for k, m in sharers:
        next_copy(k, m).wait_recv()
    mate_copy().start()
    mate_copy().wait_recv()
    second(0)
    for i in range(1, pieces):
        for a in range(group):
            feed_terms(a, i - 1)
        far_sums(i)
        second(i)

    def third(a, _):
        products[...] = lax.dot_general(
            panels_next[a], residuals_next[a], LAST_TO_LAST, preferred_element_type=F32
        )
        pick(1, a, support_all[base + a])
        twin_copy(1, a).start()

        @pl.when(a > 0)
        def _():
            forward(1, a - 1)

        return 0

    lax.fori_loop(0, group, third, 0)
    forward(1, group - 1)
    for a in range(terms_window, group):
        feed_terms(a, pieces - 1)
    reduce_codes(1)
    for j in range(1, pairs):
        row_copy(j).start()
    for j in range(1, pairs):
        row_copy(j).wait_recv()
    last_copy().start()

    def gather_terms(i, a_first, a_end, last):
        for a in range(a_first, a_end):
            for j in range(1, owners):
                term_copy(a, j, i).wait_recv()

        def one_slot(r, _):
            rows = pl.ds(pl.multiple_of(r * block_width, block_width), block_width)
            for k in range(group):
                start = k * width + i * piece_width
                if a_first:
                    total = terms[k, rows, :piece_width]
                else:
                    total = jnp.zeros((block_width, piece_width), F32)
                for h in range(groups):
                    for a in range(a_first, a_end):
                        q = h * group + a
                        total = total + same(r, q, me) * arrived[q, k, i].astype(F32)
                if last:
                    before = staged[k, r, :, i * piece_width:(i + 1) * piece_width]
                    pool[owned + r, :, start:start + piece_width] = (
                        before.astype(F32) + ATOM_RATE * total
                    ).astype(BF16)
                else:
                    terms[k, rows, :piece_width] = total
            return 0

        lax.fori_loop(0, owners, one_slot, 0)

    def place(i):
        def place_block(b, _):
            for k in range(group):
                start = k * width + i * piece_width
                dictionary_out[b, :, start:start + piece_width] = (
                    pool[chosen[b], :, start:start + piece_width]
                )
            return 0

        lax.fori_loop(0, owned, place_block, 0)

    for i in range(pieces):
        if i == pieces - 1:
            last_copy().wait_recv()
            codes_out[...] = master[...].T
            gather_terms(i, 0, group - 1, False)
            gather_terms(i, group - 1, group, True)
        else:
            gather_terms(i, 0, group, True)
        place(i)

    def drain(a, _):
        for step in range(2):
            twin_copy(step, a).wait_send()
        return 0

    lax.fori_loop(0, group, drain, 0)
    for a, i in queue[len(sent):]:
        for h in range(1, groups):
            residual_copy(a, h, i).wait_send()
    for a in range(group):
        for i in range(pieces):
            if a + terms_window >= group:
                for j in order:
                    term_copy(a, j, i).wait_send()
    for j in range(1, owners):
        for a in range(group - panels_window, group):
            panel_copy(a, j).wait_send()
        ask_copy(j).wait_send()
        support_copy(j).wait_send()
    for k in range(1, group):
        codes_copy(k).wait_send()
        near_copy(k).wait_send()
        pixel_copy(k).wait_send()
    for k, m in sharers:
        next_copy(k, m).wait_send()
        for step in range(2):
            part_copy(step, k, m).wait_send()
    for j in range(1, pairs):
        row_copy(j).wait_send()
    for h in range(1, groups):
        far_copy(h).wait_send()
        for k in range(1, group):
            fan_copy(h, k).wait_send()
        lift_copy(h).wait_send()
    mate_copy().wait_send()
    last_copy().wait_send()


def group_size(owners, pixel_count):
    group = owners // 2
    while group > 1 and (owners % group or pixel_count % (group * LANES)):
        group //= 2
    return group


def local(patterns, dictionary, codes, support, wanted):
    owners = lax.axis_size("blk")
    row_count = lax.axis_size("rows")
    pattern_rows, pixel_count = patterns.shape
    support_count = support.shape[1]
    code_width = codes.shape[1]
    block_width = code_width // support_count
    owned = dictionary.shape[0] // block_width
    scale_factor = code_width ** (-0.5)
    group = group_size(owners, pixel_count)
    groups = owners // group
    width = pixel_count // group
    pieces = 2 if width % (2 * LANES) == 0 else 1
    piece_width = width // pieces
    share = code_width // 2
    pairs = row_count // 2
    atoms = owners * block_width
    blocks = dictionary.reshape(owned, block_width, pixel_count)
    vmem = pl.BlockSpec(memory_space=pltpu.VMEM)
    hbm = pl.BlockSpec(memory_space=pltpu.HBM)
    dma = pltpu.SemaphoreType.DMA
    dictionary_after, codes_after = pl.pallas_call(
        functools.partial(steps_kernel, owners, row_count, group, pieces, block_width, scale_factor),
        out_shape=(
            jax.ShapeDtypeStruct((owned, block_width, pixel_count), BF16),
            jax.ShapeDtypeStruct((pattern_rows, code_width), F32),
        ),
        in_specs=[hbm] * 5,
        out_specs=(vmem, vmem),
        scratch_shapes=[
            pltpu.VMEM((owned + owners, block_width, pixel_count), BF16),
            pltpu.VMEM(patterns.shape, BF16),
            pltpu.VMEM(codes.shape, BF16),
            pltpu.VMEM((owners,) + support.shape[::-1], jnp.int32),
            pltpu.VMEM((owners,) + wanted.shape, jnp.int32),
            pltpu.SMEM((owners,) + wanted.shape, jnp.int32),
            pltpu.SMEM((owned,), jnp.int32),
            pltpu.VMEM((owners, code_width, pattern_rows), BF16),
            pltpu.VMEM((group, owners, block_width, width), BF16),
            pltpu.VMEM((group, owners, block_width, width), BF16),
            pltpu.VMEM((group, pattern_rows, width), BF16),
            pltpu.VMEM((group, atoms, pattern_rows), BF16),
            pltpu.VMEM((owners - group if pieces > 1 else 1, atoms, pattern_rows), BF16),
            pltpu.VMEM((owners, pieces, pattern_rows, piece_width), BF16),
            pltpu.VMEM((group, atoms, width), F32),
            pltpu.VMEM((group, atoms, width), F32),
            pltpu.VMEM((atoms, pattern_rows), F32),
            pltpu.VMEM((atoms, piece_width), F32),
            pltpu.VMEM((group, atoms, width), BF16),
            pltpu.VMEM((group, pattern_rows, width), BF16),
            pltpu.VMEM((group, pieces, owners, block_width, piece_width), BF16),
            pltpu.VMEM((owners, group, pieces, block_width, piece_width), BF16),
            pltpu.VMEM((2, group, code_width, pattern_rows), BF16),
            pltpu.VMEM((2, group, share, pattern_rows), BF16),
            pltpu.VMEM((2, group, share, pattern_rows), BF16),
            pltpu.VMEM((2, group, pairs, share // pairs, pattern_rows), BF16),
            pltpu.VMEM((code_width, pattern_rows), F32),
            pltpu.VMEM((group, code_width, pattern_rows), BF16),
            dma((6,)),
            dma((owners,)), dma((owners,)),
            dma((owners,)), dma((owners,)),
            dma((group,)), dma((group,)),
            dma((group,)), dma((group,)),
            dma((groups,)), dma((groups,)),
            dma((groups, group)), dma((groups, group)),
            dma((groups,)), dma((groups,)),
            dma((group,)), dma((group,)),
            dma((group, owners)), dma((group, owners)),
            dma((group, groups, pieces)), dma((group, groups, pieces)),
            dma((2, group)), dma((2, group)),
            dma((2, group, pairs)), dma((2, group, pairs)),
            dma((pairs,)), dma((pairs,)),
            dma((group, pairs)), dma((group, pairs)),
            dma((2,)), dma((2,)),
            dma((group, owners, pieces)), dma((group, owners, pieces)),
        ],
        compiler_params=pltpu.CompilerParams(
            collective_id=0, has_side_effects=True, vmem_limit_bytes=49 * 1024 * 1024
        ),
    )(*[pltpu.with_memory_space_constraint(x, pltpu.HBM) for x in (wanted, support.T, codes, patterns, blocks)])
    return (dictionary_after.reshape(dictionary.shape), codes_after)


def solution(mesh):
    placed = (P("blk", "rows"), P("blk", "rows"), P("blk", None), P("blk", None), P("blk", None))
    return jax.shard_map(
        local,
        mesh=mesh,
        in_specs=placed,
        out_specs=(P("blk", "rows"), P("blk", None)),
        check_vma=False,
    )
```
